256 devices in a mesh: fsdp: 32 (over y, z), rep: 8 (over x, core).
Axes of the slice: x: 4, y: 4, z: 8, core: 2. Of those that a mesh axis runs over, the one named last changes fastest.
Arguments:
- gradient: float32 [8192, 28672], P('fsdp', 'rep')
- basis: float32 [8192, 256], P('fsdp'), may hold values from -0.0625 to 0.0625
- direction: float32 [256], replicated, may hold values from -6 to 6
- first_moment: float32 [256, 28672], P('fsdp', 'rep'), may hold values from -6 to 6
- second_moment: float32 [256, 28672], P('fsdp', 'rep'), may hold values from 0.01 to 0.3
Outputs:
- update: float32 [8192, 28672], P('fsdp', 'rep')
- new_basis: float32 [8192, 256], P('fsdp')
- first_out: float32 [256, 28672], P('fsdp', 'rep')
- second_out: float32 [256, 28672], P('fsdp', 'rep')
The draws below stay inside these ranges and needn't reach their ends.
All inputs are finite; a program needn't handle non-finite values.
Results may differ from the reference program's by a relative error of at most 0.000092.
Values sent between devices are 32-bit elements; how exact they have to be, the bound alone decides.
A program may use at most 64 MiB of HBM per device.

```python
import math
import jax
import jax.numpy as jnp
from jax import lax

D = 8192
FF = 28672
R = 256


def draw_gradient(key, part):
    keys = jax.random.split(key, 3)
    rows = jnp.arange(D, dtype=jnp.float32)[:, None]
    rise = jnp.exp(jnp.log(3.0) * rows / max(D - 1, 1))
    row_scale = rise * jnp.exp(jax.random.uniform(keys[1], (D, 1), minval=0.0, maxval=jnp.log(10.0))) / 10.0
    col_scale = jnp.exp(jax.random.uniform(keys[2], (1, FF), minval=jnp.log(0.3), maxval=jnp.log(3.0)))
    base = jax.random.normal(keys[0], (D, FF))
    return (base * row_scale * col_scale).astype(jnp.float32)


def levels(stream_key, extent, pieces, least, top_value):
    level = 1.0
    for axis_at, blocks in pieces:
        heights = jax.random.uniform(jax.random.fold_in(jax.random.fold_in(stream_key, 6), axis_at), (blocks,), jnp.float32, least / len(pieces), top_value / len(pieces))
        level = level * jnp.repeat(jnp.exp(heights), extent[axis_at] // blocks).reshape((-1,) + (1,) * (len(extent) - 1 - axis_at))
    return level


def centred(key, shape, spread, bound, pieces=(), kind=jnp.bfloat16):
    result = spread * jax.random.normal(key, shape, jnp.float32)
    if pieces:
        result = result * levels(key, shape, pieces, -0.22, 0.18)
    return jnp.clip(result, -bound, bound).astype(kind)


def setup_inputs(seed: int = 0) -> dict:
    arg_keys = jax.random.split(jax.random.key(seed), 6)
    gradient = draw_gradient(jax.random.fold_in(arg_keys[5], 71), 0)
    basis = centred(arg_keys[1], (D, R), D ** -0.5, 0.0625, ((0, 32),), jnp.float32)
    direction = centred(arg_keys[2], (R,), 1.0, 6.0, (), jnp.float32)
    first_moment = centred(arg_keys[3], (R, FF), 1.0, 6.0, ((0, 32), (1, 8)), jnp.float32)
    second_moment = jnp.clip(jnp.exp(math.log(0.3) - 3.4011974 * jax.random.uniform(arg_keys[4], (R, FF), jnp.float32) ** levels(arg_keys[4], (R, FF), ((0, 32), (1, 8)), -0.2, 0.2)), 0.01, 0.3)
    return dict(gradient=gradient, basis=basis, direction=direction, first_moment=first_moment, second_moment=second_moment)


HIGH = lax.Precision.HIGHEST

def reference(gradient, basis, direction, first_moment, second_moment):
    tangent_unit = direction / jnp.sqrt(jnp.sum(direction * direction) + 1e-06)
    projected = jnp.dot(basis.T, gradient, precision=HIGH, preferred_element_type=jnp.float32)
    column_mix = jnp.dot(tangent_unit, projected, precision=HIGH)
    row_mix = jnp.dot(projected, column_mix, precision=HIGH)
    lifted = jnp.dot(gradient, column_mix, precision=HIGH) - jnp.dot(basis, row_mix, precision=HIGH)
    sigma = jnp.sqrt(jnp.sum(lifted * lifted) + 1e-06)
    pnorm = jnp.sqrt(jnp.sum(projected * projected) + 1e-06)
    theta = jnp.arctan(0.2 * sigma / pnorm)
    cosine = jnp.cos(theta)
    sine_value = jnp.sin(theta)
    basis_dir = jnp.dot(basis, tangent_unit, precision=HIGH)
    shifted = (cosine - 1.0) * basis_dir + sine_value * (lifted / sigma)
    new_basis = basis + jnp.outer(shifted, tangent_unit)
    rotation = jnp.dot(new_basis.T, basis, precision=HIGH, preferred_element_type=jnp.float32)
    new_projected = jnp.dot(new_basis.T, gradient, precision=HIGH, preferred_element_type=jnp.float32)
    first_out = 0.9 * jnp.dot(rotation, first_moment, precision=HIGH) + 0.1 * new_projected
    second_out = 0.99 * jnp.dot(rotation * rotation, second_moment, precision=HIGH) + 0.01 * new_projected * new_projected
    low_rank = first_out / (jnp.sqrt(second_out) + 1e-08)
    update = jnp.dot(new_basis, low_rank, precision=HIGH, preferred_element_type=jnp.float32)
    return (update, new_basis, first_out, second_out)
```

```python
import functools

import jax
import jax.numpy as jnp
from jax import lax
from jax.experimental import pallas as pl
from jax.experimental.pallas import tpu as pltpu
from jax.sharding import PartitionSpec as P

MESH = pl.DeviceIdType.MESH
HIGH = lax.Precision.HIGHEST
F32 = jnp.float32
NY, NZ, NR = 4, 8, 8
NF = NY * NZ
OZ = 7
NT = NY * OZ
R = 256
W = 128


def dot(a, b):
    return jnp.dot(a, b, precision=HIGH, preferred_element_type=F32)


def copy_to(src, dst, ssem, rsem, dev):
    return pltpu.make_async_remote_copy(
        src_ref=src, dst_ref=dst, send_sem=ssem, recv_sem=rsem, device_id=dev, device_id_type=MESH
    )


def columns(row):
    return jnp.transpose(jnp.broadcast_to(row, (W, row.shape[1])))


def kernel(
    grad, basis, direction, first, second,
    update, new_basis, first_out, second_out,
    part, low, az, ay, by, bz, cz, cy, call, gs, hs, vsrc, vs, ps, ss, ka, kb, kc, kd,
    msrc, mown, fown, fsrc,
    bulk_s, bulk_r, gat_s, gat_r, cz_s, cz_r, cy_s, cy_r, g_s, g_r, h_s, h_r, v_s, v_r, p_s, p_r, s_s, s_r,
    ka_s, ka_r, kb_s, kb_r, kc_s, kc_r, kd_s, kd_r, m_s, m_r, o_s, o_r,
):
    f = lax.axis_index("fsdp")
    r = lax.axis_index("rep")
    y, z = f // NZ, f % NZ
    flip = r % 2

    def yadd(a, k):
        return (a + k - 2 * k * flip + 16) % NY

    def zadd(a, k):
        return (a + k - 2 * k * flip + 16) % NZ

    def at_y(yy):
        return {"fsdp": yy * NZ + z}

    def at_z(zz):
        return {"fsdp": y * NZ + zz}

    barrier = pltpu.get_barrier_semaphore()

    def greet_f(i, c):
        pl.semaphore_signal(barrier, inc=1, device_id={"fsdp": (f + i) % NF}, device_id_type=MESH)
        return c

    def greet_r(i, c):
        pl.semaphore_signal(barrier, inc=1, device_id={"rep": (r + i) % NR}, device_id_type=MESH)
        return c

    lax.fori_loop(1, NF, greet_f, 0)
    lax.fori_loop(1, NR, greet_r, 0)

    d = direction[...]
    unit = d / jnp.sqrt(jnp.sum(d * d, axis=1, keepdims=True) + 1e-06)
    ucol = columns(unit)
    ucol2 = jnp.concatenate([ucol, ucol], axis=1)
    bt = jnp.transpose(basis[...])
    gram = dot(bt, basis[...])
    fown[0] = gram[:, 0:W]
    fown[1] = gram[:, W:]

    for i in range(NY):
        rows = pl.ds(pl.multiple_of(32 * r + 8 * i, 8), 8)
        ka[NY + i, :, 0:W] = fown[0, rows, :]
        ka[NY + i, :, W:] = fown[1, rows, :]

    for k in range(NT):
        msrc[k, 0] = first[:, W * k : W * k + W]
        msrc[k, 1] = second[:, W * k : W * k + W]

    def part_step(j, c):
        cols = pl.ds(pl.multiple_of(j * 2 * W, 2 * W), 2 * W)
        block = dot(bt, grad[:, cols])
        row = jnp.sum(ucol2 * block, axis=0, keepdims=True)
        k0, k1 = 2 * j, 2 * j + 1
        part[k0 // OZ, k0 % OZ] = block[:, 0:W]
        part[k1 // OZ, k1 % OZ] = block[:, W:]
        cz[z, pl.ds(k0, 1), :] = row[:, 0:W]
        cz[z, pl.ds(k1, 1), :] = row[:, W:]
        return c

    lax.fori_loop(0, NT // 2, part_step, 0)
    cz[z, NT:, :] = jnp.zeros((32 - NT, W), F32)

    pl.semaphore_wait(barrier, NF - 1 + NR - 1)

    def peers(kind):
        n, me = {"y": (NY, y), "z": (NZ, z), "f": (NF, f), "r": (NR, r)}[kind]

        def dev(p):
            return {"y": at_y, "z": at_z, "f": lambda q: {"fsdp": q}, "r": lambda q: {"rep": q}}[kind](p)

        return n, me, dev

    def swap(kind, slots, ssem, rsem, src=None):
        n, me, dev = peers(kind)

        def make(i, landing):
            p = (me + i) % n
            source = slots.at[me] if src is None else src(p)
            return copy_to(source, slots.at[landing(p)], ssem.at[i], rsem.at[landing(p)], dev(p))

        def start():
            def go(i, c):
                make(i, lambda p: me).start()
                return c

            lax.fori_loop(1, n, go, 0)

        def done():
            def go(i, c):
                make(i, lambda p: p).wait_recv()
                return c

            lax.fori_loop(1, n, go, 0)

        def sent():
            def go(i, c):
                make(i, lambda p: me).wait_send()
                return c

            lax.fori_loop(1, n, go, 0)

        return start, done, sent

    sends = []

    def rs_chain(add, me, n, dev, chunk, slots, base, absent):
        main, minor = n // 2, n // 2 - 1

        def send(step, forward, wait=False):
            if forward:
                dst, to, sem = add(me, main - step), add(me, 1), base + step
            else:
                dst, to, sem = add(me, step - minor), add(me, -1), base + main + step
            slot = step if forward else main + step
            one = lambda: copy_to(chunk(dst), slots.at[slot], bulk_s.at[sem], bulk_r.at[sem], dev(to))
            if wait:
                guarded(absent, dst, lambda: one().wait_send())
            else:
                guarded(absent, dst, lambda: one().start())
                sends.append(lambda: send(step, forward, True))

        def take(step, forward):
            if forward:
                dst, frm, sem = add(me, main - 1 - step), add(me, -1), base + step
            else:
                dst, frm, sem = add(me, step + 1 - minor), add(me, 1), base + main + step
            slot = step if forward else main + step

            def run():
                copy_to(chunk(dst), slots.at[slot], bulk_s.at[sem], bulk_r.at[sem], dev(frm)).wait_recv()
                accumulate(chunk(dst), slots.at[slot])

            guarded(absent, dst, run)

        return send, take

    def guarded(absent, dst, fn):
        if absent is None:
            fn()
        else:
            pl.when(dst != absent)(fn)

    def accumulate(ref, slot):
        if len(ref.shape) == 2:
            ref[...] += slot[...]
        else:
            for i in range(ref.shape[0]):
                ref[i] += slot[i]

    a_half, b_half = slice(0, W), slice(W, R)
    az_send, az_take = rs_chain(zadd, z, NZ, at_z, lambda q: part.at[:, q, a_half, :], az, 0, OZ)
    by_send, by_take = rs_chain(yadd, y, NY, at_y, lambda q: part.at[q, :, b_half, :], by, 7, None)
    ay_send, ay_take = rs_chain(yadd, y, NY, at_y, lambda q: part.at[q, z, a_half, :], ay, 10, None)
    bz_send, bz_take = rs_chain(zadd, z, NZ, at_z, lambda q: part.at[y, q, b_half, :], bz, 13, OZ)

    c_z = swap("z", cz, cz_s, cz_r)
    c_y = swap("y", cy, cy_s, cy_r)
    g_x = swap("r", gs, g_s, g_r)
    h_x = swap("f", hs, h_s, h_r)
    p_x = swap("r", ps, p_s, p_r)
    s_x = swap("f", ss, s_s, s_r)
    k_a = swap("y", ka, ka_s, ka_r, src=lambda p: ka.at[NY + p])
    k_b = swap("z", kb, kb_s, kb_r)
    k_c = swap("y", kc, kc_s, kc_r)
    k_d = swap("r", kd, kd_s, kd_r)

    c_z[0]()
    az_send(0, True)
    by_send(0, True)
    by_send(0, False)
    az_send(0, False)
    k_a[0]()

    def m_make(i, landing):
        p = (f + i) % NF
        tile = (p // NZ) * OZ + p % NZ
        rows = pl.ds(pl.multiple_of(8 * landing(p), 8), 8)
        return p, lambda: copy_to(msrc.at[tile], mown.at[:, rows, :], m_s.at[i], m_r.at[landing(p)], {"fsdp": p})

    def m_start(i, c):
        p, one = m_make(i, lambda p: f)
        pl.when(p % NZ != OZ)(lambda: one().start())
        return c

    def m_sent(i, c):
        p, one = m_make(i, lambda p: f)
        pl.when(p % NZ != OZ)(lambda: one().wait_send())
        return c

    def m_done(i, c):
        p = (f + i) % NF
        rows = pl.ds(pl.multiple_of(8 * p, 8), 8)
        copy_to(msrc.at[0], mown.at[:, rows, :], m_s.at[i], m_r.at[p], {"fsdp": p}).wait_recv()
        return c

    lax.fori_loop(1, NF, m_start, 0)
    owner = z != OZ
    tile = y * OZ + z

    c_z[1]()
    cy[y] = jnp.sum(cz[...], axis=0)
    c_y[0]()

    ka[y] = ka[NY + y]
    k_a[1]()
    kb[z] = ka[0] + ka[1] + ka[2] + ka[3]
    k_b[0]()

    az_take(0, True)
    az_send(1, True)
    az_take(0, False)
    az_send(1, False)

    c_y[1]()
    call[...] = cy[0] + cy[1] + cy[2] + cy[3]

    acc = grad[:, 0:W] * call[0:1, :]
    for k in range(1, NT):
        acc += grad[:, W * k : W * k + W] * call[k : k + 1, :]
    gs[r] = jnp.sum(jnp.transpose(acc), axis=0, keepdims=True)
    g_x[0]()

    by_take(0, True)
    by_send(1, True)
    by_take(0, False)

    g_x[1]()
    grow = jnp.sum(gs[...], axis=0)
    gcol = columns(grow)
    gcol2 = jnp.concatenate([gcol, gcol], axis=1)
    hs[f] = jnp.sum(gcol2 * basis[...], axis=0, keepdims=True)
    h_x[0]()
    for k in range(NT):
        vsrc[k] = jnp.sum(gcol * grad[:, W * k : W * k + W], axis=0, keepdims=True)

    def v_start(i, c):
        p = (f + i) % NF
        t = (p // NZ) * OZ + p % NZ

        @pl.when(p % NZ != OZ)
        def _():
            copy_to(vsrc.at[t], vs.at[f], v_s.at[i], v_r.at[f], {"fsdp": p}).start()

        return c

    def v_sent(i, c):
        p = (f + i) % NF
        t = (p // NZ) * OZ + p % NZ

        @pl.when(p % NZ != OZ)
        def _():
            copy_to(vsrc.at[t], vs.at[f], v_s.at[i], v_r.at[f], {"fsdp": p}).wait_send()

        return c

    def v_done(i, c):
        p = (f + i) % NF
        copy_to(vsrc.at[0], vs.at[p], v_s.at[i], v_r.at[p], {"fsdp": p}).wait_recv()
        return c

    lax.fori_loop(1, NF, v_start, 0)

    k_b[1]()
    kc[y] = ((kb[0] + kb[1]) + (kb[2] + kb[3])) + ((kb[4] + kb[5]) + (kb[6] + kb[7]))
    k_c[0]()

    az_take(1, True)
    az_send(2, True)
    az_take(1, False)
    az_send(2, False)
    by_take(1, True)
    bz_send(0, True)
    bz_send(0, False)
    az_take(2, True)
    az_send(3, True)
    az_take(2, False)
    k_c[1]()
    for i in range(NY):
        kd[r, 8 * i : 8 * i + 8, :] = kc[i]
    k_d[0]()

    h_x[1]()
    hrow = jnp.sum(hs[...], axis=0)
    gc = gcol[:, 0:1]
    lifted = gc - jnp.sum(basis[...] * hrow, axis=1, keepdims=True)
    sig_part = jnp.sum(lifted * lifted, axis=0, keepdims=True)

    bz_take(0, True)
    bz_send(1, True)
    bz_take(0, False)
    bz_send(1, False)
    bz_take(1, True)
    bz_send(2, True)
    bz_take(1, False)
    bz_send(2, False)
    az_take(3, True)

    def a_second():
        ay_send(0, True)
        ay_send(0, False)
        ay_take(0, True)
        ay_send(1, True)
        ay_take(0, False)
        ay_take(1, True)

    mark = len(sends)
    pl.when(owner)(a_second)
    ay_sends = sends[mark:]
    del sends[mark:]
    bz_take(2, True)
    bz_send(3, True)
    bz_take(2, False)
    bz_take(3, True)

    @pl.when(owner)
    def _():
        own = part[y, z]
        ps[r] = jnp.broadcast_to(jnp.sum(jnp.sum(own * own, axis=0, keepdims=True), axis=1, keepdims=True), (1, W))

    @pl.when(z == OZ)
    def _():
        ps[r] = jnp.zeros((1, W), F32)

    p_x[0]()
    p_x[1]()
    prow = jnp.sum(ps[...], axis=0)
    lane = lax.broadcasted_iota(jnp.int32, (1, W), 1)
    ss[f] = jnp.where(lane < W // 2, jnp.broadcast_to(sig_part, (1, W)), prow)
    s_x[0]()
    k_d[1]()
    s_x[1]()
    norms = jnp.sum(ss[...], axis=0)
    sigma = 0.2 * jnp.sqrt(norms[:, 0:1] + 1e-06)
    pnorm = jnp.sqrt(norms[:, W - 1 : W] + 1e-06)
    top = jnp.maximum(sigma, pnorm)
    opp, adj = sigma / top, pnorm / top
    hyp = jnp.sqrt(opp * opp + adj * adj)
    cos_less = -(opp * opp) / (hyp * (hyp + adj))
    sin_over = (opp / hyp) / (5.0 * sigma)

    tcol = jnp.sum(basis[...] * unit, axis=1, keepdims=True)
    shifted = cos_less * tcol + sin_over * lifted
    nb = basis[...] + shifted * unit
    new_basis[...] = nb

    @pl.when(owner)
    def _():
        lax.fori_loop(1, NF, m_done, 0)
        lax.fori_loop(1, NF, v_done, 0)
        mown[:, pl.ds(pl.multiple_of(8 * f, 8), 8), :] = msrc[tile]
        vs[f] = vsrc[tile]
        k0 = kd[...].reshape(R, R)
        ku = jnp.sum(ucol2 * k0, axis=0, keepdims=True)
        hcol = columns(hrow)
        hcol2 = jnp.concatenate([hcol, hcol], axis=1)
        kh = jnp.sum(hcol2 * k0, axis=0, keepdims=True)
        beta = cos_less * ku + sin_over * (hrow - kh)
        rot = k0 + ucol2 * beta
        own = part[y, z]
        hp = jnp.sum(hcol * own, axis=0, keepdims=True)
        cown = call[pl.ds(tile, 1), :]
        wrow = cos_less * cown + sin_over * (jnp.sum(vs[...], axis=0) - hp)
        proj = own + ucol * wrow
        fo = 0.9 * dot(rot, mown[0]) + 0.1 * proj
        so = 0.99 * dot(rot * rot, mown[1]) + 0.01 * proj * proj
        fown[0] = fo
        fown[1] = so
        low[y, z] = fo / (jnp.sqrt(so) + 1e-08)

    gsends = []

    def ag_chain(add, me, n, dev, chunk, base, absent):
        main, minor = n // 2, n // 2 - 1

        def send(step, forward, wait=False):
            org = add(me, -step) if forward else add(me, step)
            to = add(me, 1) if forward else add(me, -1)
            sem = base + step if forward else base + main + step
            one = lambda: copy_to(chunk(org), chunk(org), gat_s.at[sem], gat_r.at[sem], dev(to))
            if wait:
                guarded(absent, org, lambda: one().wait_send())
            else:
                guarded(absent, org, lambda: one().start())
                gsends.append((base == 10, lambda: send(step, forward, True)))

        def take(step, forward):
            org = add(me, -1 - step) if forward else add(me, 1 + step)
            frm = add(me, -1) if forward else add(me, 1)
            sem = base + step if forward else base + main + step
            guarded(
                absent,
                org,
                lambda: copy_to(chunk(org), chunk(org), gat_s.at[sem], gat_r.at[sem], dev(frm)).wait_recv(),
            )

        return send, take

    hz_send, hz_take = ag_chain(zadd, z, NZ, at_z, lambda q: low.at[:, q, a_half, :], 0, OZ)
    jy_send, jy_take = ag_chain(yadd, y, NY, at_y, lambda q: low.at[q, :, b_half, :], 7, None)
    hy_send, hy_take = ag_chain(yadd, y, NY, at_y, lambda q: low.at[q, z, a_half, :], 10, None)
    jz_send, jz_take = ag_chain(zadd, z, NZ, at_z, lambda q: low.at[y, q, b_half, :], 13, OZ)

    def o_make(i, to_peer):
        p = (f + i) % NF
        if to_peer:
            rows = pl.ds(pl.multiple_of(8 * p, 8), 8)
            return p, lambda: copy_to(fown.at[:, rows, :], fsrc.at[tile], o_s.at[i], o_r.at[f], {"fsdp": p})
        t = (p // NZ) * OZ + p % NZ
        rows = pl.ds(pl.multiple_of(8 * f, 8), 8)
        return p, lambda: copy_to(fown.at[:, rows, :], fsrc.at[t], o_s.at[i], o_r.at[p], {"fsdp": p})

    def o_start(i, c):
        o_make(i, True)[1]().start()
        return c

    def o_sent(i, c):
        o_make(i, True)[1]().wait_send()
        return c

    def o_done(i, c):
        p, one = o_make(i, False)
        pl.when(p % NZ != OZ)(lambda: one().wait_recv())
        return c

    @pl.when(owner)
    def _():
        hy_send(0, True)
        hy_send(0, False)

    jz_send(0, True)
    jz_send(0, False)

    @pl.when(owner)
    def _():
        lax.fori_loop(1, NF, o_start, 0)
        fsrc[tile] = fown[:, pl.ds(pl.multiple_of(8 * f, 8), 8), :]
        hy_take(0, True)
        hy_send(1, True)

    jz_take(0, True)
    jz_send(1, True)
    jz_take(0, False)
    jz_send(1, False)

    @pl.when(owner)
    def _():
        hy_take(0, False)
        hy_take(1, True)

    hz_send(0, True)
    hz_send(0, False)
    jz_take(1, True)
    jz_send(2, True)
    jz_take(1, False)
    jz_send(2, False)
    jz_take(2, True)
    jz_send(3, True)
    jz_take(2, False)
    hz_take(0, True)
    hz_send(1, True)
    hz_take(0, False)
    hz_send(1, False)
    jz_take(3, True)
    jy_send(0, True)
    jy_send(0, False)
    hz_take(1, True)
    hz_send(2, True)
    hz_take(1, False)
    hz_send(2, False)
    jy_take(0, True)
    jy_send(1, True)
    hz_take(2, True)
    hz_send(3, True)
    hz_take(2, False)
    jy_take(0, False)
    jy_take(1, True)
    hz_take(3, True)

    def update_step(j, c):
        k0, k1 = 2 * j, 2 * j + 1
        block = jnp.concatenate([low[k0 // OZ, k0 % OZ], low[k1 // OZ, k1 % OZ]], axis=1)
        cols = pl.ds(pl.multiple_of(j * 2 * W, 2 * W), 2 * W)
        update[:, cols] = dot(new_basis[...], block)
        return c

    lax.fori_loop(0, NT // 2, update_step, 0)

    lax.fori_loop(1, NF, o_done, 0)
    for k in range(NT):
        first_out[:, W * k : W * k + W] = fsrc[k, 0]
        second_out[:, W * k : W * k + W] = fsrc[k, 1]

    for x in (c_z, c_y, g_x, h_x, p_x, s_x, k_a, k_b, k_c, k_d):
        x[2]()
    lax.fori_loop(1, NF, m_sent, 0)
    lax.fori_loop(1, NF, v_sent, 0)

    for one in sends:
        one()

    @pl.when(owner)
    def _():
        for one in ay_sends:
            one()
        for mine, one in gsends:
            if mine:
                one()
        lax.fori_loop(1, NF, o_sent, 0)

    for mine, one in gsends:
        if not mine:
            one()


def per_device(gradient, basis, direction, first_moment, second_moment):
    vmem = pl.BlockSpec(memory_space=pltpu.VMEM)
    dma = pltpu.SemaphoreType.DMA
    v = lambda *shape: pltpu.VMEM(shape, F32)
    scratch = [
        v(NY, OZ, R, W), v(NY, OZ, R, W),
        v(7, NY, W, W), v(3, W, W), v(3, OZ, W, W), v(7, W, W),
        v(NZ, 32, W), v(NY, 32, W), v(32, W), v(NR, 1, R), v(NF, 1, R),
        v(NT, 1, W), v(NF, 1, W), v(NR, 1, W), v(NF, 1, W),
        v(2 * NY, 8, R), v(NZ, 8, R), v(NY, 8, R), v(NR, 32, R),
        v(NT, 2, 8, W), v(2, R, W), v(2, R, W), v(NT, 2, 8, W),
    ]
    sems = [20, 20, 20, 20, 8, 8, 4, 4, 8, 8, 32, 32, 32, 32, 8, 8, 32, 32, 4, 4, 8, 8, 4, 4, 8, 8, 32, 32, 32, 32]
    rows, cols = gradient.shape
    own = first_moment.shape
    return pl.pallas_call(
        kernel,
        out_shape=(
            jax.ShapeDtypeStruct((rows, cols), F32),
            jax.ShapeDtypeStruct((rows, R), F32),
            jax.ShapeDtypeStruct(own, F32),
            jax.ShapeDtypeStruct(own, F32),
        ),
        in_specs=[vmem] * 5,
        out_specs=(vmem,) * 4,
        scratch_shapes=scratch + [dma((n,)) for n in sems],
        compiler_params=pltpu.CompilerParams(
            collective_id=0, has_side_effects=True, vmem_limit_bytes=60 * 1024 * 1024
        ),
    )(gradient, basis, direction.reshape(1, R), first_moment, second_moment)


def solution(mesh):
    in_specs = (P("fsdp", "rep"), P("fsdp", None), P(), P("fsdp", "rep"), P("fsdp", "rep"))
    out_specs = (P("fsdp", "rep"), P("fsdp", None), P("fsdp", "rep"), P("fsdp", "rep"))
    return jax.shard_map(
        per_device, mesh=mesh, in_specs=in_specs, out_specs=out_specs, check_vma=False
    )
```

```python
import jax
import jax.numpy as jnp
from jax import lax
from jax.experimental import pallas as pl
from jax.experimental.pallas import tpu as pltpu
from jax.sharding import PartitionSpec as P

MESH = pl.DeviceIdType.MESH
HIGH = lax.Precision.HIGHEST
F32 = jnp.float32
BF16 = jnp.bfloat16
NY, NZ, NR = 4, 8, 8
NF = NY * NZ
OZ = 7
NT = NY * OZ
R = 256
W = 128
CUT = 104
VMEM_LIMIT = 28 * 1024 * 1024
LO, HI = slice(0, CUT), slice(CUT, R)

NAMES = (
    [f"am{s}{j}" for s in range(4) for j in range(4)]
    + [f"an{s}{j}" for s in range(3) for j in range(4)]
    + ["hm00", "hm10", "hn00"]
    + [f"bm{s}{j}" for s in range(2) for j in range(8)]
    + [f"bn0{j}" for j in range(8)]
    + [f"jm{s}0" for s in range(4)]
    + [f"jn{s}0" for s in range(3)]
)
INDEX = {name: i for i, name in enumerate(NAMES)}
SCATTER_ORDER = (
    "bm00", "bn00", "bm01", "bn01", "am00", "an00", "bm10", "ka00", "am01", "bm11", "an01", "cz00", "am02", "an02",
    "am03", "an03", "am10", "bm02", "an10", "cy00", "bn02", "jm00", "bm03", "bn03", "am11", "an11", "bm04", "am12",
    "bn04", "an12", "kb00", "bm05", "gx00", "am13", "an13", "bn05", "am20", "bm06", "an20", "bn06", "jm10", "bm07",
    "am21", "bn07", "an21", "am22", "bm12", "an22", "bm13", "bm14", "am23", "an23", "bm15", "am30", "kc00", "bm16",
    "am31", "am32", "bm17", "jn00", "hx00", "hm00", "jm20", "am33", "hn00", "kd00", "jn10", "hm10", "jm30", "jn20",
)
GATHER_ORDER = (
    "hm00", "jm00", "hn00", "jn00", "bm00", "am00", "an00", "bn00", "am01", "hm10", "an01", "bm01", "jm10", "bn01",
    "am02", "an02", "bm05", "jn10", "bn05", "am10", "bm10", "an10", "am11", "bm11", "am03", "bm02", "an03", "an11",
    "bn02", "jm20", "bm15", "am12", "bm06", "an12", "bn06", "jn20", "am20", "bm12", "an20", "bm03", "am21", "bn03",
    "am13", "an13", "bm16", "an21", "bm07", "jm30", "bn07", "am22", "an22", "bm13", "am30", "am31", "bm17", "am23",
    "bm04", "an23", "am32", "bn04", "am33", "bm14",
)
SCATTER_Y = (2, 1, -1, 0)
SCATTER_Z = (4, 3, -3, 2, -2, 1, -1, 0)
GATHER_Y = (0, -1, 1, -2)
GATHER_Z = (0, -1, -2, -3, -4, 1, 2, 3)


def dot(a, b):
    return jnp.dot(a, b, precision=HIGH, preferred_element_type=F32)


def halves(x):
    top = x.astype(BF16)
    return top, (x - top.astype(F32)).astype(BF16)


def dot3(a, b):
    (ah, al), (bh, bl) = a, b
    one = lambda p, q: jnp.dot(p, q, preferred_element_type=F32)
    return one(ah, bh) + (one(ah, bl) + one(al, bh))


def copy_to(src, dst, ssem, rsem, dev):
    return pltpu.make_async_remote_copy(
        src_ref=src, dst_ref=dst, send_sem=ssem, recv_sem=rsem, device_id=dev, device_id_type=MESH
    )


def columns(row):
    return jnp.transpose(jnp.broadcast_to(row, (W, row.shape[1])))


def scatter_sends():
    need = {}
    for s in range(4):
        need[f"jm{s}0"] = [f"bm1{(0, 1, 3, 5)[s]}", f"bn0{(0, 1, 3, 5)[s]}"] + ([f"jm{s - 1}0"] if s else [])
    for s in range(3):
        need[f"jn{s}0"] = [f"bm1{(2, 4, 6)[s]}", f"bn0{(2, 4, 6)[s]}"] + ([f"jn{s - 1}0"] if s else [])
    need["hm00"] = ["am30", "an20"]
    need["hm10"] = ["am31", "an21", "hm00"]
    need["hn00"] = ["am32", "an22"]
    for j in range(8):
        for s in range(2):
            need[f"bm{s}{j}"] = [f"bm{s - 1}{j}"] if s else (["cz00"] if j >= 2 else [])
        need[f"bn0{j}"] = ["cz00"] if j >= 2 else []
        if j < 4:
            for s in range(4):
                need[f"am{s}{j}"] = [f"am{s - 1}{j}"] if s else []
            for s in range(3):
                need[f"an{s}{j}"] = [f"an{s - 1}{j}"] if s else []
    return need


def gather_sends():
    need = {"hm00": [], "hn00": [], "hm10": ["hm00"]}
    for s in range(4):
        need[f"jm{s}0"] = [f"jm{s - 1}0"] if s else []
    for s in range(3):
        need[f"jn{s}0"] = [f"jn{s - 1}0"] if s else []
    first = ([], ["hm00"], ["hn00"], ["hm10"])
    for j in range(4):
        for s in range(4):
            need[f"am{s}{j}"] = [f"am{s - 1}{j}"] if s else first[j]
        for s in range(3):
            need[f"an{s}{j}"] = [f"an{s - 1}{j}"] if s else first[j]
    for j in range(8):
        here = [] if j == 0 else [f"jm{j - 1}0" if j < 5 else f"jn{j - 5}0"]
        need[f"bm0{j}"] = here
        need[f"bn0{j}"] = here
        need[f"bm1{j}"] = [f"bm0{j}"]
    return need


class Flow:
    def __init__(self, need, start):
        self.need, self.start, self.done, self.issued = need, start, set(), []

    def issue(self):
        for name, wants in self.need.items():
            if name not in self.issued and self.done.issuperset(wants):
                self.issued.append(name)
                self.start(name)

    def finished(self, name):
        self.done.add(name)
        self.issue()


def kernel(
    grad, basis, direction, first, second,
    low, new_basis, rows_out,
    part, mine, sa, sh, sb, sj, cz, cy, call, gs, hs, vsrc, vs, ps, ss, ka, kb, kc, kd, msrc, mown, fown,
    sc_s, sc_r, ga_s, ga_r, cz_s, cz_r, cy_s, cy_r, g_s, g_r, h_s, h_r, v_s, v_r, p_s, p_r, s_s, s_r,
    ka_s, ka_r, kb_s, kb_r, kc_s, kc_r, kd_s, kd_r, m_s, m_r, o_s, o_r, local_sem,
):
    f = lax.axis_index("fsdp")
    r = lax.axis_index("rep")
    y, z = f // NZ, f % NZ
    flip = r % 2
    owner = z != OZ
    tile = y * OZ + z

    def yadd(k):
        return (y + k - 2 * k * flip + 16) % NY

    def zadd(k):
        return (z + k - 2 * k * flip + 16) % NZ

    def at_y(yy):
        return {"fsdp": yy * NZ + z}

    def at_z(zz):
        return {"fsdp": y * NZ + zz}

    barrier = pltpu.get_barrier_semaphore()

    def greet_f(i, c):
        pl.semaphore_signal(barrier, inc=1, device_id={"fsdp": (f + i) % NF}, device_id_type=MESH)
        return c

    def greet_r(i, c):
        pl.semaphore_signal(barrier, inc=1, device_id={"rep": (r + i) % NR}, device_id_type=MESH)
        return c

    lax.fori_loop(1, NF, greet_f, 0)
    lax.fori_loop(1, NR, greet_r, 0)

    d = direction[...]
    unit = d / jnp.sqrt(jnp.sum(d * d, axis=1, keepdims=True) + 1e-06)
    tcol = jnp.sum(basis[...] * unit, axis=1, keepdims=True)
    twide = jnp.broadcast_to(tcol, (R, W))
    for k in range(NT):
        cz[z, k : k + 1, :] = jnp.sum(twide * grad[:, W * k : W * k + W], axis=0, keepdims=True)
    cz[z, NT:, :] = jnp.zeros((32 - NT, W), F32)

    bt = jnp.transpose(basis[...])
    bth, btl = halves(bt)

    def part_step(j, c):
        cols = pl.ds(pl.multiple_of(j * 2 * W, 2 * W), 2 * W)
        block = dot3((bth, btl), halves(grad[:, cols]))
        k0, k1 = 2 * j, 2 * j + 1
        part[k0 // OZ, k0 % OZ] = block[:, 0:W]
        part[k1 // OZ, k1 % OZ] = block[:, W:]
        return c

    lax.fori_loop(0, NT // 2, part_step, 0)
    pl.semaphore_wait(barrier, NF - 1 + NR - 1)

    def swap(kind, slots, ssem, rsem, src=None):
        n, me, dev = {
            "y": (NY, y, at_y),
            "z": (NZ, z, at_z),
            "f": (NF, f, lambda q: {"fsdp": q}),
            "r": (NR, r, lambda q: {"rep": q}),
        }[kind]

        def make(i, landing):
            p = (me + i) % n
            source = slots.at[me] if src is None else src(p)
            return copy_to(source, slots.at[landing(p)], ssem.at[i], rsem.at[landing(p)], dev(p))

        def loop(act):
            def go(i, c):
                act(i)
                return c

            lax.fori_loop(1, n, go, 0)

        return (
            lambda: loop(lambda i: make(i, lambda p: me).start()),
            lambda: loop(lambda i: make(i, lambda p: p).wait_recv()),
            lambda: loop(lambda i: make(i, lambda p: me).wait_send()),
        )

    c_z = swap("z", cz, cz_s, cz_r)
    c_y = swap("y", cy, cy_s, cy_r)
    g_x = swap("r", gs, g_s, g_r)
    h_x = swap("f", hs, h_s, h_r)
    p_x = swap("r", ps, p_s, p_r)
    s_x = swap("f", ss, s_s, s_r)
    k_a = swap("y", ka, ka_s, ka_r, src=lambda p: ka.at[NY + p])
    k_b = swap("z", kb, kb_s, kb_r)
    k_c = swap("y", kc, kc_s, kc_r)
    k_d = swap("r", kd, kd_s, kd_r)

    def spot(yy, zz, kind):
        return part.at[yy, zz, LO if kind in "ah" else HI, :]

    def slot_of(name):
        i = INDEX[name]
        for ref in (sa, sh, sb, sj):
            if i < ref.shape[0]:
                return ref.at[i]
            i -= ref.shape[0]

    def scatter_route(name):
        kind, way, s, j = name[0], name[1], int(name[2]), int(name[3])
        main = way == "m"
        if kind == "a":
            yy = yadd(SCATTER_Y[j])
            zs, zr = (zadd(4 - s), zadd(3 - s)) if main else (zadd(s - 3), zadd(s - 2))
            return (yy, zs), (yy, zr), at_z(zadd(1 if main else -1)), zs, zr
        if kind == "j":
            zs, zr = (zadd(4 - s), zadd(3 - s)) if main else (zadd(s - 3), zadd(s - 2))
            return (y, zs), (y, zr), at_z(zadd(1 if main else -1)), zs, zr
        zz = z if kind == "h" else zadd(SCATTER_Z[j])
        ys, yr = (yadd(2 - s), yadd(1 - s)) if main else (yadd(-1), y)
        return (ys, zz), (yr, zz), at_y(yadd(1 if main else -1)), zz, zz

    def scatter_copy(name, to_send):
        leave, arrive, dev, zs, zr = scatter_route(name)
        i = INDEX[name]
        where = leave if to_send else arrive
        one = lambda: copy_to(spot(*where, name[0]), slot_of(name), sc_s.at[i], sc_r.at[i], dev)
        return one, (zs if to_send else zr) != OZ, spot(*arrive, name[0])

    def scatter_start(name):
        one, there, _ = scatter_copy(name, True)
        pl.when(there)(lambda: one().start())

    def scatter_take(name):
        one, there, ref = scatter_copy(name, False)

        @pl.when(there)
        def _():
            one().wait_recv()
            ref[...] += slot_of(name)[...]

    values = {}

    def on_cz():
        c_z[1]()
        cy[y] = ((cz[0] + cz[1]) + (cz[2] + cz[3])) + ((cz[4] + cz[5]) + (cz[6] + cz[7]))
        c_y[0]()

    def on_cy():
        c_y[1]()
        call[...] = (cy[0] + cy[1]) + (cy[2] + cy[3])
        acc = grad[:, 0:W] * call[0:1, :]
        for k in range(1, NT):
            acc += grad[:, W * k : W * k + W] * call[k : k + 1, :]
        gs[r] = jnp.sum(jnp.transpose(acc), axis=0, keepdims=True)
        g_x[0]()

    def v_copy(i, p):
        t = (p // NZ) * OZ + p % NZ
        return copy_to(vsrc.at[t], vs.at[f], v_s.at[i], v_r.at[f], {"fsdp": p})

    def v_start(i, c):
        p = (f + i) % NF
        pl.when(p % NZ != OZ)(lambda: v_copy(i, p).start())
        return c

    def v_sent(i, c):
        p = (f + i) % NF
        pl.when(p % NZ != OZ)(lambda: v_copy(i, p).wait_send())
        return c

    def v_done(i, c):
        p = (f + i) % NF
        copy_to(vsrc.at[0], vs.at[p], v_s.at[i], v_r.at[p], {"fsdp": p}).wait_recv()
        return c

    def on_gx():
        g_x[1]()
        gcol = columns(jnp.sum(gs[...], axis=0))
        values["g"] = gcol
        hs[f] = jnp.sum(jnp.concatenate([gcol, gcol], axis=1) * basis[...], axis=0, keepdims=True)
        h_x[0]()
        for k in range(NT):
            vsrc[k] = jnp.sum(gcol * grad[:, W * k : W * k + W], axis=0, keepdims=True)
        lax.fori_loop(1, NF, v_start, 0)

    def on_hx():
        h_x[1]()
        hrow = jnp.sum(hs[...], axis=0)
        lifted = values["g"][:, 0:1] - jnp.sum(basis[...] * hrow, axis=1, keepdims=True)
        values["h"], values["lifted"] = hrow, lifted
        values["sig"] = jnp.sum(lifted * lifted, axis=0, keepdims=True)

    def on_ka():
        ka[y] = ka[NY + y]
        k_a[1]()
        kb[z] = (ka[0] + ka[1]) + (ka[2] + ka[3])
        k_b[0]()

    def on_kb():
        k_b[1]()
        kc[y] = ((kb[0] + kb[1]) + (kb[2] + kb[3])) + ((kb[4] + kb[5]) + (kb[6] + kb[7]))
        k_c[0]()

    def on_kc():
        k_c[1]()
        for i in range(NY):
            kd[r, 8 * i : 8 * i + 8, :] = kc[i]
        k_d[0]()

    chain = {
        "cz00": on_cz, "cy00": on_cy, "gx00": on_gx, "hx00": on_hx,
        "ka00": on_ka, "kb00": on_kb, "kc00": on_kc, "kd00": k_d[1],
    }

    c_z[0]()
    scatter = Flow(scatter_sends(), scatter_start)
    scatter.issue()

    gram = dot(bt, basis[...])
    fown[0] = gram[:, 0:W]
    fown[1] = gram[:, W:]
    for i in range(NY):
        rows = pl.ds(pl.multiple_of(32 * r + 8 * i, 8), 8)
        ka[NY + i, :, 0:W] = fown[0, rows, :]
        ka[NY + i, :, W:] = fown[1, rows, :]
    k_a[0]()

    for k in range(NT):
        msrc[k, 0] = first[:, W * k : W * k + W]
        msrc[k, 1] = second[:, W * k : W * k + W]

    for name in SCATTER_ORDER:
        if name in chain:
            chain[name]()
        else:
            scatter_take(name)
        scatter.finished(name)

    @pl.when(owner)
    def _():
        own = part[y, z]
        ps[r] = jnp.broadcast_to(jnp.sum(jnp.sum(own * own, axis=0, keepdims=True), axis=1, keepdims=True), (1, W))

    @pl.when(z == OZ)
    def _():
        ps[r] = jnp.zeros((1, W), F32)

    p_x[0]()

    def m_copy(i, p):
        rows = pl.ds(pl.multiple_of(8 * f, 8), 8)
        t = (p // NZ) * OZ + p % NZ
        return copy_to(msrc.at[t], mown.at[:, rows, :], m_s.at[i], m_r.at[f], {"fsdp": p})

    def m_start(i, c):
        p = (f + i) % NF
        pl.when(p % NZ != OZ)(lambda: m_copy(i, p).start())
        return c

    def m_sent(i, c):
        p = (f + i) % NF
        pl.when(p % NZ != OZ)(lambda: m_copy(i, p).wait_send())
        return c

    def m_done(i, c):
        p = (f + i) % NF
        rows = pl.ds(pl.multiple_of(8 * p, 8), 8)
        copy_to(msrc.at[0], mown.at[:, rows, :], m_s.at[i], m_r.at[p], {"fsdp": p}).wait_recv()
        return c

    lax.fori_loop(1, NF, m_start, 0)

    p_x[1]()
    prow = jnp.sum(ps[...], axis=0)
    lane = lax.broadcasted_iota(jnp.int32, (1, W), 1)
    ss[f] = jnp.where(lane < W // 2, jnp.broadcast_to(values["sig"], (1, W)), prow)
    s_x[0]()

    @pl.when(owner)
    def _():
        lax.fori_loop(1, NF, v_done, 0)
        lax.fori_loop(1, NF, m_done, 0)
        mown[:, pl.ds(pl.multiple_of(8 * f, 8), 8), :] = msrc[tile]
        vs[f] = vsrc[tile]

    s_x[1]()
    norms = jnp.sum(ss[...], axis=0)
    opposite = 0.2 * jnp.sqrt(norms[:, 0:1] + 1e-06)
    adjacent = jnp.sqrt(norms[:, W - 1 : W] + 1e-06)
    top = jnp.maximum(opposite, adjacent)
    opp, adj = opposite / top, adjacent / top
    hyp = jnp.sqrt(opp * opp + adj * adj)
    cos_less = -(opp * opp) / (hyp * (hyp + adj))
    sin_over = (opp / hyp) / (5.0 * opposite)
    hrow, lifted = values["h"], values["lifted"]

    @pl.when(owner)
    def _():
        ucol = columns(unit)
        ucol2 = jnp.concatenate([ucol, ucol], axis=1)
        k0 = kd[...].reshape(R, R)
        ku = jnp.sum(ucol2 * k0, axis=0, keepdims=True)
        hcol = columns(hrow)
        hcol2 = jnp.concatenate([hcol, hcol], axis=1)
        kh = jnp.sum(hcol2 * k0, axis=0, keepdims=True)
        beta = cos_less * ku + sin_over * (hrow - kh)
        rot = k0 + ucol2 * beta
        own = part[y, z]
        hp = jnp.sum(hcol * own, axis=0, keepdims=True)
        cown = call[pl.ds(tile, 1), :]
        wrow = cos_less * cown + sin_over * (jnp.sum(vs[...], axis=0) - hp)
        proj = own + ucol * wrow
        fo = 0.9 * dot(rot, mown[0]) + 0.1 * proj
        so = 0.99 * dot(rot * rot, mown[1]) + 0.01 * proj * proj
        fown[0] = fo
        fown[1] = so
        mine[...] = fo / (jnp.sqrt(so) + 1e-08)

    def gather_route(name):
        kind, way, s, j = name[0], name[1], int(name[2]), int(name[3])
        main = way == "m"
        if kind in "aj":
            yy = yadd(GATHER_Y[j]) if kind == "a" else y
            zs, zr = (zadd(-s), zadd(-1 - s)) if main else (zadd(s), zadd(1 + s))
            own = s == 0 and (kind == "j" or j == 0)
            return (yy, zs), (yy, zr), at_z(zadd(1 if main else -1)), own
        zz = z if kind == "h" else zadd(GATHER_Z[j])
        ys, yr = (yadd(-s), yadd(-1 - s)) if main else (y, yadd(1))
        own = s == 0 and (kind == "h" or j == 0)
        return (ys, zz), (yr, zz), at_y(yadd(1 if main else -1)), own

    def gather_copy(name, to_send):
        leave, arrive, dev, own = gather_route(name)
        i = INDEX[name]
        rows = LO if name[0] in "ah" else HI
        yy, zz = leave if to_send else arrive

        def one():
            dst = low.at[yy, zz, rows, :]
            src = mine.at[rows, :] if own and to_send else dst
            return copy_to(src, dst, ga_s.at[i], ga_r.at[i], dev)

        return one, zz != OZ

    def gather_start(name):
        one, there = gather_copy(name, True)
        pl.when(there)(lambda: one().start())

    def gather_take(name):
        one, there = gather_copy(name, False)
        pl.when(there)(lambda: one().wait_recv())

    gather = Flow(gather_sends(), gather_start)
    gather.issue()

    own_rows = pl.ds(pl.multiple_of(8 * f, 8), 8)
    keep_low = lambda: pltpu.make_async_copy(mine, low.at[y, z], local_sem.at[0])
    keep_rows = lambda: pltpu.make_async_copy(fown.at[:, own_rows, :], rows_out.at[tile], local_sem.at[1])

    @pl.when(owner)
    def _():
        keep_low().start()
        keep_rows().start()

    new_basis[...] = basis[...] + (cos_less * tcol + sin_over * lifted) * unit

    def o_copy(i, p):
        rows = pl.ds(pl.multiple_of(8 * p, 8), 8)
        return copy_to(fown.at[:, rows, :], rows_out.at[tile], o_s.at[i], o_r.at[f], {"fsdp": p})

    def o_start(i, c):
        o_copy(i, (f + i) % NF).start()
        return c

    def o_sent(i, c):
        o_copy(i, (f + i) % NF).wait_send()
        return c

    def o_done(i, c):
        p = (f + i) % NF
        t = (p // NZ) * OZ + p % NZ
        one = lambda: copy_to(fown.at[:, own_rows, :], rows_out.at[t], o_s.at[i], o_r.at[p], {"fsdp": p})
        pl.when(p % NZ != OZ)(lambda: one().wait_recv())
        return c

    def send_rows():
        lax.fori_loop(1, NF, o_start, 0)

    for at, name in enumerate(GATHER_ORDER):
        if at == len(GATHER_ORDER) // 2:
            pl.when(owner)(send_rows)
        gather_take(name)
        gather.finished(name)

    lax.fori_loop(1, NF, o_done, 0)

    for x in (c_z, c_y, g_x, h_x, p_x, s_x, k_a, k_b, k_c, k_d):
        x[2]()
    lax.fori_loop(1, NF, m_sent, 0)
    lax.fori_loop(1, NF, v_sent, 0)
    for flow, make in ((scatter, scatter_copy), (gather, gather_copy)):
        for name in flow.issued:
            one, there = make(name, True)[:2]
            pl.when(there)(lambda one=one: one().wait_send())

    @pl.when(owner)
    def _():
        lax.fori_loop(1, NF, o_sent, 0)
        keep_low().wait()
        keep_rows().wait()


def finish_kernel(nb, low, rows, update, new_basis, first_out, second_out):
    left = halves(nb[...])
    for i in range(low.shape[0] // 2):
        block = jnp.concatenate([low[2 * i], low[2 * i + 1]], axis=1)
        update[:, 2 * W * i : 2 * W * (i + 1)] = dot3(left, halves(block))

    @pl.when(pl.program_id(0) == 0)
    def _():
        new_basis[...] = nb[...]
        for k in range(NT):
            first_out[:, W * k : W * k + W] = rows[k, 0]
            second_out[:, W * k : W * k + W] = rows[k, 1]


def per_device(gradient, basis, direction, first_moment, second_moment):
    vmem = pl.BlockSpec(memory_space=pltpu.VMEM)
    anywhere = pl.BlockSpec(memory_space=pl.ANY)
    dma = pltpu.SemaphoreType.DMA
    v = lambda *shape: pltpu.VMEM(shape, F32)
    shape = lambda *s: jax.ShapeDtypeStruct(s, F32)
    scratch = [
        v(NY, OZ, R, W), v(R, W),
        v(28, CUT, W), v(3, CUT, W), v(24, R - CUT, W), v(7, R - CUT, W),
        v(NZ, 32, W), v(NY, 32, W), v(32, W), v(NR, 1, R), v(NF, 1, R),
        v(NT, 1, W), v(NF, 1, W), v(NR, 1, W), v(NF, 1, W),
        v(2 * NY, 8, R), v(NZ, 8, R), v(NY, 8, R), v(NR, 32, R),
        v(NT, 2, 8, W), v(2, R, W), v(2, R, W),
    ]
    n = len(NAMES)
    sems = [n, n, n, n, 8, 8, 4, 4, 8, 8, 32, 32, 32, 32, 8, 8, 32, 32, 4, 4, 8, 8, 4, 4, 8, 8, 32, 32, 32, 32, 2]
    rows, cols = gradient.shape
    own = first_moment.shape
    low, nb, moved = pl.pallas_call(
        kernel,
        out_shape=(shape(NY, OZ, R, W), shape(rows, R), shape(NT, 2, 8, W)),
        in_specs=[vmem] * 5,
        out_specs=(anywhere, vmem, anywhere),
        scratch_shapes=scratch + [dma((k,)) for k in sems],
        compiler_params=pltpu.CompilerParams(
            collective_id=0, has_side_effects=True, vmem_limit_bytes=VMEM_LIMIT
        ),
    )(gradient, basis, direction.reshape(1, R), first_moment, second_moment)
    per = 4
    whole = lambda *s: pl.BlockSpec(s, lambda i: (0,) * len(s))
    return pl.pallas_call(
        finish_kernel,
        grid=(NT // per,),
        out_shape=(shape(rows, cols), shape(rows, R), shape(*own), shape(*own)),
        in_specs=[whole(rows, R), pl.BlockSpec((per, R, W), lambda i: (i, 0, 0)), whole(NT, 2, 8, W)],
        out_specs=(pl.BlockSpec((rows, per * W), lambda i: (0, i)), whole(rows, R), whole(*own), whole(*own)),
        compiler_params=pltpu.CompilerParams(vmem_limit_bytes=12 * 1024 * 1024),
    )(nb, low.reshape(NT, R, W), moved)


def solution(mesh):
    in_specs = (P("fsdp", "rep"), P("fsdp", None), P(), P("fsdp", "rep"), P("fsdp", "rep"))
    out_specs = (P("fsdp", "rep"), P("fsdp", None), P("fsdp", "rep"), P("fsdp", "rep"))
    return jax.shard_map(
        per_device, mesh=mesh, in_specs=in_specs, out_specs=out_specs, check_vma=False
    )
```

```python
import jax
import jax.numpy as jnp
from jax import lax
from jax.experimental import pallas as pl
from jax.experimental.pallas import tpu as pltpu
from jax.sharding import PartitionSpec as P

MESH = pl.DeviceIdType.MESH
HIGH = lax.Precision.HIGHEST
F32 = jnp.float32
BF16 = jnp.bfloat16
NY, NZ, NR = 4, 8, 8
NF = NY * NZ
OZ = 7
PER = 4
NT = NY * OZ
R = 256
W = 128
CUT = 96
VMEM_LIMIT = 28 * 1024 * 1024
LO, HI = slice(0, CUT), slice(CUT, R)

NAMES = (
    [f"am{s}{j}" for s in range(4) for j in range(4)]
    + [f"an{s}{j}" for s in range(3) for j in range(4)]
    + ["hm00", "hm10", "hn00"]
    + [f"bm{s}{j}" for s in range(2) for j in range(8)]
    + [f"bn0{j}" for j in range(8)]
    + [f"jm{s}0" for s in range(4)]
    + [f"jn{s}0" for s in range(3)]
)
INDEX = {name: i for i, name in enumerate(NAMES)}
SCATTER_ORDER = (
    "bm00", "bn00", "bm01", "am00", "bn01", "an00", "bm02", "am01", "an01", "bn02", "cz00", "am02", "bm03", "an02",
    "bn03", "am03", "an03", "ka00", "bm10", "am10", "an10", "bm11", "am11", "bm12", "an11", "am12", "an12", "bm04",
    "am13", "cy00", "bn04", "an13", "bm05", "jm00", "bn05", "am20", "bm06", "an20", "kb00", "am21", "bn06", "jn00",
    "bm07", "an21", "bn07", "am22", "an22", "bm13", "am23", "bm14", "gx00", "an23", "bm15", "jm10", "bm16", "am30",
    "am31", "kc00", "bm17", "am32", "am33", "hm00", "jn10", "hn00", "jm20", "hm10", "jn20", "jm30", "hx00", "kd00",
)
GATHER_ORDER = (
    "hm00", "jm00", "hn00", "jn00", "bm00", "am00", "an00", "bn00", "am01", "hm10", "an01", "bm01", "jm10", "bn01",
    "am02", "an02", "bm05", "jn10", "bn05", "am10", "an10", "bm10", "am11", "bm11", "am03", "an03", "bm02", "an11",
    "bn02", "jm20", "am12", "bm15", "an12", "bm06", "jn20", "bn06", "am20", "an20", "bm12", "am21", "am13", "bm03",
    "an13", "bn03", "an21", "jm30", "am22", "bm16", "bm07", "bn07", "an22", "bm13", "am30", "am31", "bm04", "am23",
    "bn04", "an23", "am32", "bm17", "bm14", "am33",
)
SCATTER_Y = (2, 1, -1, 0)
SCATTER_Z = (4, 3, -3, 2, -2, 1, -1, 0)
GATHER_Y = (0, -1, 1, -2)
GATHER_Z = (0, -1, -2, -3, -4, 1, 2, 3)


def dot(a, b):
    return jnp.dot(a, b, precision=HIGH, preferred_element_type=F32)


def halves(x):
    top = x.astype(BF16)
    return top, (x - top.astype(F32)).astype(BF16)


def dot3(a, b):
    (ah, al), (bh, bl) = a, b
    one = lambda p, q: jnp.dot(p, q, preferred_element_type=F32)
    return one(ah, bh) + (one(ah, bl) + one(al, bh))


def copy_to(src, dst, ssem, rsem, dev):
    return pltpu.make_async_remote_copy(
        src_ref=src, dst_ref=dst, send_sem=ssem, recv_sem=rsem, device_id=dev, device_id_type=MESH
    )


def columns(row):
    return jnp.transpose(jnp.broadcast_to(row, (W, row.shape[1])))


def scatter_sends():
    need = {}
    for s in range(4):
        need[f"jm{s}0"] = [f"bm1{(0, 1, 3, 5)[s]}", f"bn0{(0, 1, 3, 5)[s]}"] + ([f"jm{s - 1}0"] if s else [])
    for s in range(3):
        need[f"jn{s}0"] = [f"bm1{(2, 4, 6)[s]}", f"bn0{(2, 4, 6)[s]}"] + ([f"jn{s - 1}0"] if s else [])
    need["hm00"] = ["am30", "an20"]
    need["hm10"] = ["am31", "an21", "hm00"]
    need["hn00"] = ["am32", "an22"]
    for j in range(8):
        for s in range(2):
            need[f"bm{s}{j}"] = [f"bm{s - 1}{j}"] if s else (["cz00"] if j >= 4 else [])
        need[f"bn0{j}"] = ["cz00"] if j >= 4 else []
        if j < 4:
            for s in range(4):
                need[f"am{s}{j}"] = [f"am{s - 1}{j}"] if s else []
            for s in range(3):
                need[f"an{s}{j}"] = [f"an{s - 1}{j}"] if s else []
    return need


def gather_sends():
    need = {"hm00": [], "hn00": [], "hm10": ["hm00"]}
    for s in range(4):
        need[f"jm{s}0"] = [f"jm{s - 1}0"] if s else []
    for s in range(3):
        need[f"jn{s}0"] = [f"jn{s - 1}0"] if s else []
    first = ([], ["hm00"], ["hn00"], ["hm10"])
    for j in range(4):
        for s in range(4):
            need[f"am{s}{j}"] = [f"am{s - 1}{j}"] if s else first[j]
        for s in range(3):
            need[f"an{s}{j}"] = [f"an{s - 1}{j}"] if s else first[j]
    for j in range(8):
        here = [] if j == 0 else [f"jm{j - 1}0" if j < 5 else f"jn{j - 5}0"]
        need[f"bm0{j}"] = here
        need[f"bn0{j}"] = here
        need[f"bm1{j}"] = [f"bm0{j}"]
    return need


class Flow:
    def __init__(self, need, start):
        self.need, self.start, self.done, self.issued = need, start, set(), []

    def issue(self):
        for name, wants in self.need.items():
            if name not in self.issued and self.done.issuperset(wants):
                self.issued.append(name)
                self.start(name)

    def finished(self, name):
        self.done.add(name)
        self.issue()


def kernel(
    grad_in, basis_in, direction_in, first_in, second_in,
    low, new_basis, rows_out,
    grad, basis, direction, first, second, part, mine, sa, sh, sb, sj, cz, cy, call, gs, hs, vsrc, vs, ps, ss, ka, kb, kc, kd, msrc, mown, fown,
    bulk_s, bulk_r, small_s, small_r, local_sem,
):
    f = lax.axis_index("fsdp")
    r = lax.axis_index("rep")
    y, z = f // NZ, f % NZ
    flip = r % 2
    owner = z != OZ
    tile = y * OZ + z

    def yadd(k):
        return (y + k - 2 * k * flip + 16) % NY

    def zadd(k):
        return (z + k - 2 * k * flip + 16) % NZ

    def at_y(yy):
        return {"fsdp": yy * NZ + z}

    def at_z(zz):
        return {"fsdp": y * NZ + zz}

    loads = [
        pltpu.make_async_copy(src, dst, local_sem.at[i])
        for i, (src, dst) in enumerate(
            ((direction_in, direction), (basis_in, basis), (first_in, first), (second_in, second))
        )
    ]
    slab = OZ * W
    loads += [
        pltpu.make_async_copy(
            grad_in.at[:, slab * i : slab * (i + 1)], grad.at[:, slab * i : slab * (i + 1)], local_sem.at[4 + i]
        )
        for i in range(NY)
    ]
    for i in (0, 1, 4, 5, 6, 7, 2, 3):
        loads[i].start()

    barrier = pltpu.get_barrier_semaphore()

    def greet_f(i, c):
        pl.semaphore_signal(barrier, inc=1, device_id={"fsdp": (f + i) % NF}, device_id_type=MESH)
        return c

    def greet_r(i, c):
        pl.semaphore_signal(barrier, inc=1, device_id={"rep": (r + i) % NR}, device_id_type=MESH)
        return c

    lax.fori_loop(1, NF, greet_f, 0)
    lax.fori_loop(1, NR, greet_r, 0)

    loads[0].wait()
    loads[1].wait()
    d = direction[...]
    unit = d / jnp.sqrt(jnp.sum(d * d, axis=1, keepdims=True) + 1e-06)
    tcol = jnp.sum(basis[...] * unit, axis=1, keepdims=True)
    twide = jnp.broadcast_to(tcol, (R, W))
    for k in range(NT):
        if k % OZ == 0:
            loads[4 + k // OZ].wait()
        cz[z, k : k + 1, :] = jnp.sum(twide * grad[:, W * k : W * k + W], axis=0, keepdims=True)
    cz[z, NT:, :] = jnp.zeros((32 - NT, W), F32)

    bt = jnp.transpose(basis[...])
    bth, btl = halves(bt)

    def part_step(j, c):
        cols = pl.ds(pl.multiple_of(j * 2 * W, 2 * W), 2 * W)
        block = dot3((bth, btl), halves(grad[:, cols]))
        k0, k1 = 2 * j, 2 * j + 1
        part[k0 // OZ, k0 % OZ] = block[:, 0:W]
        part[k1 // OZ, k1 % OZ] = block[:, W:]
        return c

    lax.fori_loop(0, NT // 2, part_step, 0)
    pl.semaphore_wait(barrier, NF - 1 + NR - 1)

    def wait_all(ref, sem):
        pltpu.make_async_copy(ref, ref, sem).wait()

    def peers(kind):
        return {
            "y": (NY, y, at_y),
            "z": (NZ, z, at_z),
            "f": (NF, f, lambda q: {"fsdp": q}),
            "r": (NR, r, lambda q: {"rep": q}),
        }[kind]

    count = [0]

    def swap(kind, slots, src=None):
        n, me, dev = peers(kind)
        ssem, rsem = small_s.at[count[0]], small_r.at[count[0]]
        count[0] += 1

        def start():
            def go(i, c):
                p = (me + i) % n
                source = slots.at[me] if src is None else src(p)
                copy_to(source, slots.at[me], ssem, rsem, dev(p)).start()
                return c

            lax.fori_loop(1, n, go, 0)

        others = slots.at[pl.ds(0, n - 1)]
        return start, lambda: wait_all(others, rsem), lambda: wait_all(others, ssem)

    c_z = swap("z", cz)
    c_y = swap("y", cy)
    g_x = swap("r", gs)
    h_x = swap("f", hs)
    p_x = swap("r", ps)
    s_x = swap("f", ss)
    k_a = swap("y", ka, src=lambda p: ka.at[NY + p])
    k_b = swap("z", kb)
    k_c = swap("y", kc)
    k_d = swap("r", kd)
    v_s, v_r, m_s, m_r, o_s, o_r = (x.at[10 + i] for i in range(3) for x in (small_s, small_r))

    def owners_but_me(ref, sem):
        pl.when(owner)(lambda: wait_all(ref.at[pl.ds(0, NT - 1)], sem))
        pl.when(z == OZ)(lambda: wait_all(ref.at[pl.ds(0, NT)], sem))

    def spot(yy, zz, kind):
        return part.at[yy, zz, LO if kind in "ah" else HI, :]

    def slot_of(name):
        i = INDEX[name]
        for ref in (sa, sh, sb, sj):
            if i < ref.shape[0]:
                return ref.at[i]
            i -= ref.shape[0]

    def scatter_route(name):
        kind, way, s, j = name[0], name[1], int(name[2]), int(name[3])
        main = way == "m"
        if kind == "a":
            yy = yadd(SCATTER_Y[j])
            zs, zr = (zadd(4 - s), zadd(3 - s)) if main else (zadd(s - 3), zadd(s - 2))
            return (yy, zs), (yy, zr), at_z(zadd(1 if main else -1)), zs, zr
        if kind == "j":
            zs, zr = (zadd(4 - s), zadd(3 - s)) if main else (zadd(s - 3), zadd(s - 2))
            return (y, zs), (y, zr), at_z(zadd(1 if main else -1)), zs, zr
        zz = z if kind == "h" else zadd(SCATTER_Z[j])
        ys, yr = (yadd(2 - s), yadd(1 - s)) if main else (yadd(-1), y)
        return (ys, zz), (yr, zz), at_y(yadd(1 if main else -1)), zz, zz

    def scatter_copy(name, to_send):
        leave, arrive, dev, zs, zr = scatter_route(name)
        i = INDEX[name]
        where = leave if to_send else arrive
        one = lambda: copy_to(spot(*where, name[0]), slot_of(name), bulk_s.at[i], bulk_r.at[i], dev)
        return one, (zs if to_send else zr) != OZ, spot(*arrive, name[0])

    def scatter_start(name):
        one, there, _ = scatter_copy(name, True)
        pl.when(there)(lambda: one().start())

    def scatter_take(name):
        one, there, ref = scatter_copy(name, False)

        @pl.when(there)
        def _():
            one().wait_recv()
            ref[...] += slot_of(name)[...]

    values = {}

    def on_cz():
        c_z[1]()
        cy[y] = ((cz[0] + cz[1]) + (cz[2] + cz[3])) + ((cz[4] + cz[5]) + (cz[6] + cz[7]))
        c_y[0]()

    def on_cy():
        c_y[1]()
        call[...] = (cy[0] + cy[1]) + (cy[2] + cy[3])
        acc = grad[:, 0:W] * call[0:1, :]
        for k in range(1, NT):
            acc += grad[:, W * k : W * k + W] * call[k : k + 1, :]
        gs[r] = jnp.sum(jnp.transpose(acc), axis=0, keepdims=True)
        g_x[0]()

    def v_start(i, c):
        p = (f + i) % NF
        t = (p // NZ) * OZ + p % NZ
        pl.when(p % NZ != OZ)(lambda: copy_to(vsrc.at[t], vs.at[f], v_s, v_r, {"fsdp": p}).start())
        return c

    def on_gx():
        g_x[1]()
        gcol = columns(jnp.sum(gs[...], axis=0))
        values["g"] = gcol
        hs[f] = jnp.sum(jnp.concatenate([gcol, gcol], axis=1) * basis[...], axis=0, keepdims=True)
        h_x[0]()
        for k in range(NT):
            vsrc[k] = jnp.sum(gcol * grad[:, W * k : W * k + W], axis=0, keepdims=True)
        lax.fori_loop(1, NF, v_start, 0)

    def on_hx():
        h_x[1]()
        hrow = jnp.sum(hs[...], axis=0)
        lifted = values["g"][:, 0:1] - jnp.sum(basis[...] * hrow, axis=1, keepdims=True)
        values["h"], values["lifted"] = hrow, lifted
        values["sig"] = jnp.sum(lifted * lifted, axis=0, keepdims=True)

    def on_ka():
        ka[y] = ka[NY + y]
        k_a[1]()
        kb[z] = (ka[0] + ka[1]) + (ka[2] + ka[3])
        k_b[0]()

    def on_kb():
        k_b[1]()
        kc[y] = ((kb[0] + kb[1]) + (kb[2] + kb[3])) + ((kb[4] + kb[5]) + (kb[6] + kb[7]))
        k_c[0]()

    def on_kc():
        k_c[1]()
        for i in range(NY):
            kd[r, 8 * i : 8 * i + 8, :] = kc[i]
        k_d[0]()

    def m_start(i, c):
        p = (f + i) % NF
        t = (p // NZ) * OZ + p % NZ
        rows = pl.ds(pl.multiple_of(8 * f, 8), 8)
        pl.when(p % NZ != OZ)(lambda: copy_to(msrc.at[t], mown.at[:, rows, :], m_s, m_r, {"fsdp": p}).start())
        return c

    chain = {
        "cz00": on_cz, "cy00": on_cy, "gx00": on_gx, "hx00": on_hx,
        "ka00": on_ka, "kb00": on_kb, "kc00": on_kc, "kd00": k_d[1],
    }

    c_z[0]()
    scatter = Flow(scatter_sends(), scatter_start)
    scatter.issue()

    gram = dot(bt, basis[...])
    fown[0] = gram[:, 0:W]
    fown[1] = gram[:, W:]
    for i in range(NY):
        rows = pl.ds(pl.multiple_of(32 * r + 8 * i, 8), 8)
        ka[NY + i, :, 0:W] = fown[0, rows, :]
        ka[NY + i, :, W:] = fown[1, rows, :]
    k_a[0]()

    loads[2].wait()
    loads[3].wait()
    for k in range(NT):
        msrc[k, 0] = first[:, W * k : W * k + W]
        msrc[k, 1] = second[:, W * k : W * k + W]

    for name in SCATTER_ORDER:
        if name in chain:
            chain[name]()
        else:
            scatter_take(name)
        scatter.finished(name)

    @pl.when(owner)
    def _():
        own = part[y, z]
        ps[r] = jnp.broadcast_to(jnp.sum(jnp.sum(own * own, axis=0, keepdims=True), axis=1, keepdims=True), (1, W))

    @pl.when(z == OZ)
    def _():
        ps[r] = jnp.zeros((1, W), F32)

    p_x[0]()
    lax.fori_loop(1, NF, m_start, 0)

    p_x[1]()
    prow = jnp.sum(ps[...], axis=0)
    lane = lax.broadcasted_iota(jnp.int32, (1, W), 1)
    ss[f] = jnp.where(lane < W // 2, jnp.broadcast_to(values["sig"], (1, W)), prow)
    s_x[0]()

    for x in (c_z, c_y, g_x, h_x, k_a, k_b, k_c, k_d):
        x[2]()
    for name in scatter.issued:
        one, there = scatter_copy(name, True)[:2]
        pl.when(there)(lambda one=one: one().wait_send())
    owners_but_me(vsrc, v_s)
    owners_but_me(msrc, m_s)

    @pl.when(owner)
    def _():
        wait_all(vs.at[pl.ds(0, NF - 1)], v_r)
        wait_all(mown.at[:, pl.ds(0, R - 8), :], m_r)
        mown[:, pl.ds(pl.multiple_of(8 * f, 8), 8), :] = msrc[tile]
        vs[f] = vsrc[tile]

    s_x[1]()
    norms = jnp.sum(ss[...], axis=0)
    opposite = 0.2 * jnp.sqrt(norms[:, 0:1] + 1e-06)
    adjacent = jnp.sqrt(norms[:, W - 1 : W] + 1e-06)
    top = jnp.maximum(opposite, adjacent)
    opp, adj = opposite / top, adjacent / top
    hyp = jnp.sqrt(opp * opp + adj * adj)
    cos_less = -(opp * opp) / (hyp * (hyp + adj))
    sin_over = (opp / hyp) / (5.0 * opposite)
    hrow, lifted = values["h"], values["lifted"]

    @pl.when(owner)
    def _():
        ucol = columns(unit)
        ucol2 = jnp.concatenate([ucol, ucol], axis=1)
        k0 = kd[...].reshape(R, R)
        ku = jnp.sum(ucol2 * k0, axis=0, keepdims=True)
        hcol = columns(hrow)
        hcol2 = jnp.concatenate([hcol, hcol], axis=1)
        kh = jnp.sum(hcol2 * k0, axis=0, keepdims=True)
        beta = cos_less * ku + sin_over * (hrow - kh)
        rot = k0 + ucol2 * beta
        own = part[y, z]
        hp = jnp.sum(hcol * own, axis=0, keepdims=True)
        cown = call[pl.ds(tile, 1), :]
        wrow = cos_less * cown + sin_over * (jnp.sum(vs[...], axis=0) - hp)
        proj = own + ucol * wrow
        fo = 0.9 * dot(rot, mown[0]) + 0.1 * proj
        so = 0.99 * dot(rot * rot, mown[1]) + 0.01 * proj * proj
        fown[0] = fo
        fown[1] = so
        mine[...] = fo / (jnp.sqrt(so) + 1e-08)

    def gather_route(name):
        kind, way, s, j = name[0], name[1], int(name[2]), int(name[3])
        main = way == "m"
        if kind in "aj":
            yy = yadd(GATHER_Y[j]) if kind == "a" else y
            zs, zr = (zadd(-s), zadd(-1 - s)) if main else (zadd(s), zadd(1 + s))
            own = s == 0 and (kind == "j" or j == 0)
            return (yy, zs), (yy, zr), at_z(zadd(1 if main else -1)), own
        zz = z if kind == "h" else zadd(GATHER_Z[j])
        ys, yr = (yadd(-s), yadd(-1 - s)) if main else (y, yadd(1))
        own = s == 0 and (kind == "h" or j == 0)
        return (ys, zz), (yr, zz), at_y(yadd(1 if main else -1)), own

    def gather_copy(name, to_send):
        leave, arrive, dev, own = gather_route(name)
        i = INDEX[name]
        rows = LO if name[0] in "ah" else HI
        yy, zz = leave if to_send else arrive

        def one():
            dst = low.at[yy, zz, rows, :]
            src = mine.at[rows, :] if own and to_send else dst
            return copy_to(src, dst, bulk_s.at[i], bulk_r.at[i], dev)

        return one, zz != OZ

    def gather_start(name):
        one, there = gather_copy(name, True)
        pl.when(there)(lambda: one().start())

    def gather_take(name):
        one, there = gather_copy(name, False)
        pl.when(there)(lambda: one().wait_recv())

    gather = Flow(gather_sends(), gather_start)
    gather.issue()

    own_rows = pl.ds(pl.multiple_of(8 * f, 8), 8)
    keep_low = lambda: pltpu.make_async_copy(mine, low.at[y, z], local_sem.at[8])
    keep_rows = lambda: pltpu.make_async_copy(fown.at[:, own_rows, :], rows_out.at[tile], local_sem.at[9])

    @pl.when(owner)
    def _():
        keep_low().start()
        keep_rows().start()

    new_basis[...] = basis[...] + (cos_less * tcol + sin_over * lifted) * unit

    def o_start(i, c):
        p = (f + i) % NF
        rows = pl.ds(pl.multiple_of(8 * p, 8), 8)
        copy_to(fown.at[:, rows, :], rows_out.at[tile], o_s, o_r, {"fsdp": p}).start()
        return c

    def send_rows():
        lax.fori_loop(1, NF, o_start, 0)

    for at, name in enumerate(GATHER_ORDER):
        if at == len(GATHER_ORDER) // 2:
            pl.when(owner)(send_rows)
        gather_take(name)
        gather.finished(name)

    owners_but_me(rows_out, o_r)

    p_x[2]()
    s_x[2]()
    for name in gather.issued:
        one, there = gather_copy(name, True)
        pl.when(there)(lambda one=one: one().wait_send())

    @pl.when(owner)
    def _():
        wait_all(fown.at[:, pl.ds(0, R - 8), :], o_s)
        keep_low().wait()
        keep_rows().wait()


def finish_kernel(nb, low, rows, update, new_basis, first_out, second_out):
    left = halves(nb[...])
    at = pl.program_id(0) * PER
    for i in range(PER // 2):
        block = jnp.concatenate([low[at + 2 * i], low[at + 2 * i + 1]], axis=1)
        update[:, 2 * W * i : 2 * W * (i + 1)] = dot3(left, halves(block))

    @pl.when(pl.program_id(0) == 0)
    def _():
        new_basis[...] = nb[...]
        for k in range(NT):
            first_out[:, W * k : W * k + W] = rows[k, 0]
            second_out[:, W * k : W * k + W] = rows[k, 1]


def per_device(gradient, basis, direction, first_moment, second_moment):
    vmem = pl.BlockSpec(memory_space=pltpu.VMEM)
    anywhere = pl.BlockSpec(memory_space=pl.ANY)
    dma = pltpu.SemaphoreType.DMA
    v = lambda *shape: pltpu.VMEM(shape, F32)
    shape = lambda *s: jax.ShapeDtypeStruct(s, F32)
    rows, cols = gradient.shape
    own = first_moment.shape
    scratch = [
        v(rows, cols), v(rows, R), v(1, R), v(*own), v(*own),
        v(NY, OZ, R, W), v(R, W),
        v(28, CUT, W), v(3, CUT, W), v(24, R - CUT, W), v(7, R - CUT, W),
        v(NZ, 32, W), v(NY, 32, W), v(32, W), v(NR, 1, R), v(NF, 1, R),
        v(NT, 1, W), v(NF, 1, W), v(NR, 1, W), v(NF, 1, W),
        v(2 * NY, 8, R), v(NZ, 8, R), v(NY, 8, R), v(NR, 32, R),
        v(NT, 2, 8, W), v(2, R, W), v(2, R, W),
    ]
    sems = [len(NAMES), len(NAMES), 13, 13, 10]
    arrays = (gradient, basis, direction.reshape(1, R), first_moment, second_moment)
    low, nb, moved = pl.pallas_call(
        kernel,
        out_shape=(shape(NY, OZ, R, W), shape(rows, R), shape(NT, 2, 8, W)),
        in_specs=[pl.BlockSpec(memory_space=pltpu.HBM)] * 5,
        out_specs=(anywhere, vmem, anywhere),
        scratch_shapes=scratch + [dma((k,)) for k in sems],
        compiler_params=pltpu.CompilerParams(
            collective_id=0, has_side_effects=True, vmem_limit_bytes=VMEM_LIMIT
        ),
    )(*(pltpu.with_memory_space_constraint(x, pltpu.HBM) for x in arrays))
    whole = lambda *s: pl.BlockSpec(s, lambda i: (0,) * len(s))
    return pl.pallas_call(
        finish_kernel,
        grid=(NT // PER,),
        out_shape=(shape(rows, cols), shape(rows, R), shape(*own), shape(*own)),
        in_specs=[vmem] * 3,
        out_specs=(pl.BlockSpec((rows, PER * W), lambda i: (0, i)), whole(rows, R), whole(*own), whole(*own)),
        compiler_params=pltpu.CompilerParams(vmem_limit_bytes=12 * 1024 * 1024),
    )(nb, low.reshape(NT, R, W), moved)


def solution(mesh):
    in_specs = (P("fsdp", "rep"), P("fsdp", None), P(), P("fsdp", "rep"), P("fsdp", "rep"))
    out_specs = (P("fsdp", "rep"), P("fsdp", None), P("fsdp", "rep"), P("fsdp", "rep"))
    return jax.shard_map(
        per_device, mesh=mesh, in_specs=in_specs, out_specs=out_specs, check_vma=False
    )
```

```python
import jax
import jax.numpy as jnp
from jax import lax
from jax.experimental import pallas as pl
from jax.experimental.pallas import tpu as pltpu
from jax.sharding import PartitionSpec as P

MESH = pl.DeviceIdType.MESH
HIGH = lax.Precision.HIGHEST
F32 = jnp.float32
BF16 = jnp.bfloat16
NY, NZ, NR = 4, 8, 8
NF = NY * NZ
OZ = 7
PER = 4
NT = NY * OZ
R = 256
W = 128
CUT = 96
VMEM_LIMIT = 28 * 1024 * 1024
LO, HI = slice(0, CUT), slice(CUT, R)

NAMES = (
    [f"am{s}{j}" for s in range(4) for j in range(4)]
    + [f"an{s}{j}" for s in range(3) for j in range(4)]
    + ["hm00", "hm10", "hn00"]
    + [f"bm{s}{j}" for s in range(2) for j in range(8)]
    + [f"bn0{j}" for j in range(8)]
    + [f"jm{s}0" for s in range(4)]
    + [f"jn{s}0" for s in range(3)]
)
INDEX = {name: i for i, name in enumerate(NAMES)}
SCATTER_ORDER = (
    "bm00", "am00", "an00", "bn00", "am01", "bm01", "an01", "am02", "bn01", "an02", "bm02", "am03", "an03", "bn02",
    "cz00", "am10", "bm03", "an10", "am11", "bn03", "an11", "ka00", "am12", "bm10", "an12", "bm11", "am13", "bm12",
    "an13", "am20", "bm04", "an20", "am21", "bn04", "an21", "bm05", "am22", "bn05", "jm00", "cy00", "bm06", "an22",
    "am23", "bn06", "kb00", "jn00", "bm07", "an23", "bn07", "am30", "am31", "bm13", "am32", "bm14", "jm10", "bm15",
    "am33", "bm16", "bm17", "jn10", "gx00", "hm00", "jm20", "hn00", "kr00", "jn20", "hm10", "jm30",
)
GATHER_ORDER = (
    "hm00", "jm00", "hn00", "jn00", "bm00", "am00", "an00", "bn00", "am01", "hm10", "an01", "bm01", "jm10", "bn01",
    "am02", "an02", "bm05", "jn10", "bn05", "am10", "an10", "bm10", "am11", "bm11", "am03", "an03", "bm02", "an11",
    "bn02", "jm20", "am12", "bm15", "an12", "bm06", "jn20", "bn06", "am20", "an20", "bm12", "am21", "am13", "bm03",
    "an13", "bn03", "an21", "jm30", "am22", "bm16", "bm07", "bn07", "an22", "bm13", "am30", "am31", "bm04", "am23",
    "an23", "bn04", "am32", "bm17", "am33", "bm14",
)
SCATTER_Y = (2, 1, -1, 0)
SCATTER_Z = (4, 3, -3, 2, -2, 1, -1, 0)
GATHER_Y = (0, -1, 1, -2)
GATHER_Z = (0, -1, -2, -3, -4, 1, 2, 3)


def dot(a, b):
    return jnp.dot(a, b, precision=HIGH, preferred_element_type=F32)


def halves(x):
    top = x.astype(BF16)
    return top, (x - top.astype(F32)).astype(BF16)


def dot3(a, b):
    (ah, al), (bh, bl) = a, b
    one = lambda p, q: jnp.dot(p, q, preferred_element_type=F32)
    return one(ah, bh) + (one(ah, bl) + one(al, bh))


def copy_to(src, dst, ssem, rsem, dev):
    return pltpu.make_async_remote_copy(
        src_ref=src, dst_ref=dst, send_sem=ssem, recv_sem=rsem, device_id=dev, device_id_type=MESH
    )


def columns(row):
    return jnp.transpose(jnp.broadcast_to(row, (W, row.shape[1])))


def scatter_sends():
    need = {}
    for s in range(4):
        need[f"jm{s}0"] = [f"bm1{(0, 1, 3, 5)[s]}", f"bn0{(0, 1, 3, 5)[s]}"] + ([f"jm{s - 1}0"] if s else [])
    for s in range(3):
        need[f"jn{s}0"] = [f"bm1{(2, 4, 6)[s]}", f"bn0{(2, 4, 6)[s]}"] + ([f"jn{s - 1}0"] if s else [])
    need["hm00"] = ["am30", "an20"]
    need["hm10"] = ["am31", "an21", "hm00"]
    need["hn00"] = ["am32", "an22"]
    for j in range(8):
        for s in range(2):
            need[f"bm{s}{j}"] = [f"bm{s - 1}{j}"] if s else [f"P{j}"] + (["cz00"] if j >= 4 else [])
        need[f"bn0{j}"] = [f"P{j}"] + (["cz00"] if j >= 4 else [])
        if j < 4:
            for s in range(4):
                need[f"am{s}{j}"] = [f"am{s - 1}{j}"] if s else ["P0"]
            for s in range(3):
                need[f"an{s}{j}"] = [f"an{s - 1}{j}"] if s else ["P2"]
    return need


def gather_sends():
    need = {"hm00": [], "hn00": [], "hm10": ["hm00"]}
    for s in range(4):
        need[f"jm{s}0"] = [f"jm{s - 1}0"] if s else []
    for s in range(3):
        need[f"jn{s}0"] = [f"jn{s - 1}0"] if s else []
    first = ([], ["hm00"], ["hn00"], ["hm10"])
    for j in range(4):
        for s in range(4):
            need[f"am{s}{j}"] = [f"am{s - 1}{j}"] if s else first[j]
        for s in range(3):
            need[f"an{s}{j}"] = [f"an{s - 1}{j}"] if s else first[j]
    for j in range(8):
        here = [] if j == 0 else [f"jm{j - 1}0" if j < 5 else f"jn{j - 5}0"]
        need[f"bm0{j}"] = here
        need[f"bn0{j}"] = here
        need[f"bm1{j}"] = [f"bm0{j}"]
    return need


class Flow:
    def __init__(self, need, start):
        self.need, self.start, self.done, self.issued = need, start, set(), []

    def issue(self):
        for name, wants in self.need.items():
            if name not in self.issued and self.done.issuperset(wants):
                self.issued.append(name)
                self.start(name)

    def finished(self, name):
        self.done.add(name)
        self.issue()


def kernel(
    grad_in, basis_in, direction_in, first_in, second_in,
    low, new_basis, rows_out,
    grad, basis, direction, first, second, part, mine, sa, sh, sb, sj, csrc, cz, call, gs, hs, vsrc, vs, ps, ss, ka, ksum, kb, kr, kc, kd, msrc, mown, fown,
    bulk_s, bulk_r, small_s, small_r, local_sem,
):
    f = lax.axis_index("fsdp")
    r = lax.axis_index("rep")
    y, z = f // NZ, f % NZ
    flip = r % 2
    owner = z != OZ
    tile = y * OZ + z

    def yadd(k):
        return (y + k - 2 * k * flip + 16) % NY

    def zadd(k):
        return (z + k - 2 * k * flip + 16) % NZ

    def at_y(yy):
        return {"fsdp": yy * NZ + z}

    def at_z(zz):
        return {"fsdp": y * NZ + zz}

    loads = [
        pltpu.make_async_copy(src, dst, local_sem.at[i])
        for i, (src, dst) in enumerate(
            ((direction_in, direction), (basis_in, basis), (first_in, first), (second_in, second))
        )
    ]
    slab = OZ * W
    loads += [
        pltpu.make_async_copy(
            grad_in.at[:, slab * i : slab * (i + 1)], grad.at[:, slab * i : slab * (i + 1)], local_sem.at[4 + i]
        )
        for i in range(NY)
    ]
    for i in (0, 1, 4, 5, 6, 7, 2, 3):
        loads[i].start()

    barrier = pltpu.get_barrier_semaphore()

    def greet_f(i, c):
        pl.semaphore_signal(barrier, inc=1, device_id={"fsdp": (f + i) % NF}, device_id_type=MESH)
        return c

    def greet_r(i, c):
        pl.semaphore_signal(barrier, inc=1, device_id={"rep": (r + i) % NR}, device_id_type=MESH)
        return c

    lax.fori_loop(1, NF, greet_f, 0)
    lax.fori_loop(1, NR, greet_r, 0)

    loads[0].wait()
    loads[1].wait()
    d = direction[...]
    unit = d / jnp.sqrt(jnp.sum(d * d, axis=1, keepdims=True) + 1e-06)
    tcol = jnp.sum(basis[...] * unit, axis=1, keepdims=True)
    twide = jnp.broadcast_to(tcol, (R, W))
    for k in range(NT):
        if k % OZ == 0:
            loads[4 + k // OZ].wait()
        csrc[k] = jnp.sum(twide * grad[:, W * k : W * k + W], axis=0, keepdims=True)

    bt = jnp.transpose(basis[...])
    bth, btl = halves(bt)

    def part_pair(y0, y1, zz):
        cols = lambda yy: pl.ds(pl.multiple_of((yy * OZ + zz) * W, W), W)

        @pl.when(zz != OZ)
        def _():
            block = dot3((bth, btl), halves(jnp.concatenate([grad[:, cols(y0)], grad[:, cols(y1)]], axis=1)))
            part[y0, zz] = block[:, 0:W]
            part[y1, zz] = block[:, W:]

    def part_column(k):
        def go(i, c):
            part_pair(yadd(2 - i), yadd(i - 1), zadd(k))
            return c

        lax.fori_loop(0, 2, go, 0)

    pl.semaphore_wait(barrier, NF - 1 + NR - 1)

    def wait_all(ref, sem):
        pltpu.make_async_copy(ref, ref, sem).wait()

    def peers(kind):
        return {
            "y": (NY, y, at_y),
            "z": (NZ, z, at_z),
            "f": (NF, f, lambda q: {"fsdp": q}),
            "r": (NR, r, lambda q: {"rep": q}),
        }[kind]

    count = [0]

    def swap(kind, slots, src=None):
        n, me, dev = peers(kind)
        ssem, rsem = small_s.at[count[0]], small_r.at[count[0]]
        count[0] += 1

        def start():
            def go(i, c):
                p = (me + i) % n
                source = slots.at[me] if src is None else src(p)
                copy_to(source, slots.at[me], ssem, rsem, dev(p)).start()
                return c

            lax.fori_loop(1, n, go, 0)

        others = slots.at[pl.ds(0, n - 1)]
        return start, lambda: wait_all(others, rsem), lambda: wait_all(others, ssem)

    g_x = swap("r", gs)
    h_x = swap("f", hs)
    p_x = swap("r", ps)
    s_x = swap("f", ss)
    k_a = swap("y", ka, src=lambda p: ka.at[NY + p])
    k_b = swap("z", kb, src=lambda p: ksum.at[p])
    k_r = swap("z", kr)
    k_c = swap("y", kc)
    k_d = swap("r", kd)
    v_s, v_r, m_s, m_r, o_s, o_r, c_s, c_r, d_s, d_r = (x.at[9 + i] for i in range(5) for x in (small_s, small_r))

    def owners_but_me(ref, sem):
        pl.when(owner)(lambda: wait_all(ref.at[pl.ds(0, NT - 1)], sem))
        pl.when(z == OZ)(lambda: wait_all(ref.at[pl.ds(0, NT)], sem))

    def spot(yy, zz, kind):
        return part.at[yy, zz, LO if kind in "ah" else HI, :]

    def slot_of(name):
        i = INDEX[name]
        for ref in (sa, sh, sb, sj):
            if i < ref.shape[0]:
                return ref.at[i]
            i -= ref.shape[0]

    def scatter_route(name):
        kind, way, s, j = name[0], name[1], int(name[2]), int(name[3])
        main = way == "m"
        if kind == "a":
            yy = yadd(SCATTER_Y[j])
            zs, zr = (zadd(4 - s), zadd(3 - s)) if main else (zadd(s - 3), zadd(s - 2))
            return (yy, zs), (yy, zr), at_z(zadd(1 if main else -1)), zs, zr
        if kind == "j":
            zs, zr = (zadd(4 - s), zadd(3 - s)) if main else (zadd(s - 3), zadd(s - 2))
            return (y, zs), (y, zr), at_z(zadd(1 if main else -1)), zs, zr
        zz = z if kind == "h" else zadd(SCATTER_Z[j])
        ys, yr = (yadd(2 - s), yadd(1 - s)) if main else (yadd(-1), y)
        return (ys, zz), (yr, zz), at_y(yadd(1 if main else -1)), zz, zz

    def scatter_copy(name, to_send):
        leave, arrive, dev, zs, zr = scatter_route(name)
        i = INDEX[name]
        where = leave if to_send else arrive
        one = lambda: copy_to(spot(*where, name[0]), slot_of(name), bulk_s.at[i], bulk_r.at[i], dev)
        return one, (zs if to_send else zr) != OZ, spot(*arrive, name[0])

    def scatter_start(name):
        one, there, _ = scatter_copy(name, True)
        pl.when(there)(lambda: one().start())

    def scatter_take(name):
        one, there, ref = scatter_copy(name, False)

        @pl.when(there)
        def _():
            one().wait_recv()
            ref[...] += slot_of(name)[...]

    values = {}

    def c_start(i, c):
        p = (f + i) % NF
        t = (p // NZ) * OZ + p % NZ
        pl.when(p % NZ != OZ)(lambda: copy_to(csrc.at[t], cz.at[f], c_s, c_r, {"fsdp": p}).start())
        return c

    def d_start(i, c):
        copy_to(call.at[tile], call.at[tile], d_s, d_r, {"fsdp": (f + i) % NF}).start()
        return c

    def on_cz():
        @pl.when(owner)
        def _():
            wait_all(cz.at[pl.ds(0, NF - 1)], c_r)
            cz[f] = csrc[tile]
            call[tile] = jnp.sum(cz[...], axis=0)
            lax.fori_loop(1, NF, d_start, 0)

    def on_cy():
        owners_but_me(call, d_r)
        acc = grad[:, 0:W] * call[0]
        for k in range(1, NT):
            acc += grad[:, W * k : W * k + W] * call[k]
        gs[r] = jnp.sum(jnp.transpose(acc), axis=0, keepdims=True)
        g_x[0]()

    def v_start(i, c):
        p = (f + i) % NF
        t = (p // NZ) * OZ + p % NZ
        pl.when(p % NZ != OZ)(lambda: copy_to(vsrc.at[t], vs.at[f], v_s, v_r, {"fsdp": p}).start())
        return c

    def on_gx():
        g_x[1]()
        gcol = columns(jnp.sum(gs[...], axis=0))
        values["g"] = gcol
        hs[f] = jnp.sum(jnp.concatenate([gcol, gcol], axis=1) * basis[...], axis=0, keepdims=True)
        h_x[0]()
        for k in range(NT):
            vsrc[k] = jnp.sum(gcol * grad[:, W * k : W * k + W], axis=0, keepdims=True)
        lax.fori_loop(1, NF, v_start, 0)

    def on_hx():
        h_x[1]()
        hrow = jnp.sum(hs[...], axis=0)
        lifted = values["g"][:, 0:1] - jnp.sum(basis[...] * hrow, axis=1, keepdims=True)
        values["h"], values["lifted"] = hrow, lifted
        values["sig"] = jnp.sum(lifted * lifted, axis=0, keepdims=True)

    def on_ka():
        ka[y] = ka[NY + y]
        k_a[1]()
        rows = (ka[0] + ka[1]) + (ka[2] + ka[3])
        for i in range(NZ):
            ksum[i] = rows[i : i + 1, :]
        k_b[0]()

    def on_kb():
        kb[z] = ksum[z]
        k_b[1]()
        kr[z] = jnp.sum(kb[...], axis=0)
        k_r[0]()

    def on_kr():
        k_r[1]()
        for i in range(NZ):
            kc[y, i : i + 1, :] = kr[i]
        k_c[0]()

    def on_kc():
        k_c[1]()
        for i in range(NY):
            kd[r, 8 * i : 8 * i + 8, :] = kc[i]
        k_d[0]()

    def m_start(i, c):
        p = (f + i) % NF
        t = (p // NZ) * OZ + p % NZ
        rows = pl.ds(pl.multiple_of(8 * f, 8), 8)
        pl.when(p % NZ != OZ)(lambda: copy_to(msrc.at[t], mown.at[:, rows, :], m_s, m_r, {"fsdp": p}).start())
        return c

    chain = {
        "cz00": on_cz, "cy00": on_cy, "gx00": on_gx,
        "ka00": on_ka, "kb00": on_kb, "kr00": on_kr,
    }

    lax.fori_loop(1, NF, c_start, 0)
    scatter = Flow(scatter_sends(), scatter_start)
    part_column(4)
    scatter.finished("P0")
    part_column(-3)
    scatter.finished("P2")
    for j in (1, 3, 4, 5, 6, 7):
        part_pair(yadd(2), yadd(-1), zadd(SCATTER_Z[j]))
        scatter.finished(f"P{j}")

    def part_rest(i, c):
        part_pair(yadd(1), y, zadd(3 - i))
        return c

    lax.fori_loop(0, 6, part_rest, 0)

    gram = dot(bt, basis[...])
    fown[0] = gram[:, 0:W]
    fown[1] = gram[:, W:]
    for i in range(NY):
        rows = pl.ds(pl.multiple_of(32 * r + 8 * i, 8), 8)
        ka[NY + i, :, 0:W] = fown[0, rows, :]
        ka[NY + i, :, W:] = fown[1, rows, :]
    k_a[0]()

    loads[2].wait()
    loads[3].wait()
    for k in range(NT):
        msrc[k, 0] = first[:, W * k : W * k + W]
        msrc[k, 1] = second[:, W * k : W * k + W]

    def spread(step, size, fn):
        low_end, high_end = 1 + step * size, min(1 + (step + 1) * size, NF)
        if step >= 0 and low_end < high_end:
            lax.fori_loop(low_end, high_end, fn, 0)

    for at, name in enumerate(SCATTER_ORDER):
        if name in chain:
            chain[name]()
        else:
            scatter_take(name)
        scatter.finished(name)

    @pl.when(owner)
    def _():
        own = part[y, z]
        ps[r] = jnp.broadcast_to(jnp.sum(jnp.sum(own * own, axis=0, keepdims=True), axis=1, keepdims=True), (1, W))

    @pl.when(z == OZ)
    def _():
        ps[r] = jnp.zeros((1, W), F32)

    p_x[0]()
    on_kc()
    lax.fori_loop(1, NF, m_start, 0)
    on_hx()

    p_x[1]()
    prow = jnp.sum(ps[...], axis=0)
    lane = lax.broadcasted_iota(jnp.int32, (1, W), 1)
    ss[f] = jnp.where(lane < W // 2, jnp.broadcast_to(values["sig"], (1, W)), prow)
    s_x[0]()
    k_d[1]()

    for x in (g_x, h_x, k_a, k_b, k_r, k_c, k_d):
        x[2]()
    for name in scatter.issued:
        one, there = scatter_copy(name, True)[:2]
        pl.when(there)(lambda one=one: one().wait_send())
    owners_but_me(csrc, c_s)
    pl.when(owner)(lambda: wait_all(cz.at[pl.ds(0, NF - 1)], d_s))
    owners_but_me(vsrc, v_s)
    owners_but_me(msrc, m_s)

    @pl.when(owner)
    def _():
        wait_all(vs.at[pl.ds(0, NF - 1)], v_r)
        wait_all(mown.at[:, pl.ds(0, R - 8), :], m_r)
        mown[:, pl.ds(pl.multiple_of(8 * f, 8), 8), :] = msrc[tile]
        vs[f] = vsrc[tile]

    s_x[1]()
    norms = jnp.sum(ss[...], axis=0)
    opposite = 0.2 * jnp.sqrt(norms[:, 0:1] + 1e-06)
    adjacent = jnp.sqrt(norms[:, W - 1 : W] + 1e-06)
    top = jnp.maximum(opposite, adjacent)
    opp, adj = opposite / top, adjacent / top
    hyp = jnp.sqrt(opp * opp + adj * adj)
    cos_less = -(opp * opp) / (hyp * (hyp + adj))
    sin_over = (opp / hyp) / (5.0 * opposite)
    hrow, lifted = values["h"], values["lifted"]

    @pl.when(owner)
    def _():
        ucol = columns(unit)
        ucol2 = jnp.concatenate([ucol, ucol], axis=1)
        k0 = kd[...].reshape(R, R)
        ku = jnp.sum(ucol2 * k0, axis=0, keepdims=True)
        hcol = columns(hrow)
        hcol2 = jnp.concatenate([hcol, hcol], axis=1)
        kh = jnp.sum(hcol2 * k0, axis=0, keepdims=True)
        beta = cos_less * ku + sin_over * (hrow - kh)
        rot = k0 + ucol2 * beta
        own = part[y, z]
        hp = jnp.sum(hcol * own, axis=0, keepdims=True)
        cown = call[tile]
        wrow = cos_less * cown + sin_over * (jnp.sum(vs[...], axis=0) - hp)
        proj = own + ucol * wrow
        fo = 0.9 * dot(rot, mown[0]) + 0.1 * proj
        so = 0.99 * dot(rot * rot, mown[1]) + 0.01 * proj * proj
        fown[1] = so
        mine[...] = fo / (jnp.sqrt(so) + 1e-08)

    def gather_route(name):
        kind, way, s, j = name[0], name[1], int(name[2]), int(name[3])
        main = way == "m"
        if kind in "aj":
            yy = yadd(GATHER_Y[j]) if kind == "a" else y
            zs, zr = (zadd(-s), zadd(-1 - s)) if main else (zadd(s), zadd(1 + s))
            own = s == 0 and (kind == "j" or j == 0)
            return (yy, zs), (yy, zr), at_z(zadd(1 if main else -1)), own
        zz = z if kind == "h" else zadd(GATHER_Z[j])
        ys, yr = (yadd(-s), yadd(-1 - s)) if main else (y, yadd(1))
        own = s == 0 and (kind == "h" or j == 0)
        return (ys, zz), (yr, zz), at_y(yadd(1 if main else -1)), own

    def gather_copy(name, to_send):
        leave, arrive, dev, own = gather_route(name)
        i = INDEX[name]
        rows = LO if name[0] in "ah" else HI
        yy, zz = leave if to_send else arrive

        def one():
            dst = low.at[yy, zz, rows, :]
            src = mine.at[rows, :] if own and to_send else dst
            return copy_to(src, dst, bulk_s.at[i], bulk_r.at[i], dev)

        return one, zz != OZ

    def gather_start(name):
        one, there = gather_copy(name, True)
        pl.when(there)(lambda: one().start())

    def gather_take(name):
        one, there = gather_copy(name, False)
        pl.when(there)(lambda: one().wait_recv())

    gather = Flow(gather_sends(), gather_start)
    gather.issue()

    own_rows = pl.ds(pl.multiple_of(8 * f, 8), 8)
    keep_low = lambda: pltpu.make_async_copy(mine, low.at[y, z], local_sem.at[8])
    keep_rows = lambda: pltpu.make_async_copy(fown.at[1, own_rows, :], rows_out.at[tile], local_sem.at[9])

    @pl.when(owner)
    def _():
        keep_low().start()
        keep_rows().start()

    new_basis[...] = basis[...] + (cos_less * tcol + sin_over * lifted) * unit

    def o_start(i, c):
        p = (f + i) % NF
        rows = pl.ds(pl.multiple_of(8 * p, 8), 8)
        copy_to(fown.at[1, rows, :], rows_out.at[tile], o_s, o_r, {"fsdp": p}).start()
        return c

    for at, name in enumerate(GATHER_ORDER):
        gather_take(name)
        gather.finished(name)
        if at >= 10:
            pl.when(owner)(lambda: spread(at - 10, 1, o_start))

    owners_but_me(rows_out, o_r)

    p_x[2]()
    s_x[2]()
    for name in gather.issued:
        one, there = gather_copy(name, True)
        pl.when(there)(lambda one=one: one().wait_send())

    @pl.when(owner)
    def _():
        wait_all(fown.at[1, pl.ds(0, R - 8), :], o_s)
        keep_low().wait()
        keep_rows().wait()


def finish_kernel(nb, low, rows, update, new_basis, first_out, second_out):
    left = halves(nb[...])
    at = pl.program_id(0) * PER
    for i in range(PER // 2):
        block = jnp.concatenate([low[at + 2 * i], low[at + 2 * i + 1]], axis=1)
        update[:, 2 * W * i : 2 * W * (i + 1)] = dot3(left, halves(block))

    @pl.when(pl.program_id(0) == 0)
    def _():
        new_basis[...] = nb[...]
        own = pl.ds(pl.multiple_of(8 * lax.axis_index("fsdp"), 8), 8)
        for k in range(NT):
            first_out[:, W * k : W * k + W] = low[k, own, :] * (jnp.sqrt(rows[k]) + 1e-08)
            second_out[:, W * k : W * k + W] = rows[k]


def per_device(gradient, basis, direction, first_moment, second_moment):
    vmem = pl.BlockSpec(memory_space=pltpu.VMEM)
    anywhere = pl.BlockSpec(memory_space=pl.ANY)
    dma = pltpu.SemaphoreType.DMA
    v = lambda *shape: pltpu.VMEM(shape, F32)
    shape = lambda *s: jax.ShapeDtypeStruct(s, F32)
    rows, cols = gradient.shape
    own = first_moment.shape
    scratch = [
        v(rows, cols), v(rows, R), v(1, R), v(*own), v(*own),
        v(NY, OZ, R, W), v(R, W),
        v(28, CUT, W), v(3, CUT, W), v(24, R - CUT, W), v(7, R - CUT, W),
        v(NT, 1, W), v(NF, 1, W), v(NT, 1, W), v(NR, 1, R), v(NF, 1, R),
        v(NT, 1, W), v(NF, 1, W), v(NR, 1, W), v(NF, 1, W),
        v(2 * NY, 8, R), v(NZ, 1, R), v(NZ, 1, R), v(NZ, 1, R), v(NY, 8, R), v(NR, 32, R),
        v(NT, 2, 8, W), v(2, R, W), v(2, R, W),
    ]
    sems = [len(NAMES), len(NAMES), 14, 14, 10]
    arrays = (gradient, basis, direction.reshape(1, R), first_moment, second_moment)
    low, nb, moved = pl.pallas_call(
        kernel,
        out_shape=(shape(NY, OZ, R, W), shape(rows, R), shape(NT, 8, W)),
        in_specs=[pl.BlockSpec(memory_space=pltpu.HBM)] * 5,
        out_specs=(anywhere, vmem, anywhere),
        scratch_shapes=scratch + [dma((k,)) for k in sems],
        compiler_params=pltpu.CompilerParams(
            collective_id=0, has_side_effects=True, vmem_limit_bytes=VMEM_LIMIT
        ),
    )(*(pltpu.with_memory_space_constraint(x, pltpu.HBM) for x in arrays))
    whole = lambda *s: pl.BlockSpec(s, lambda i: (0,) * len(s))
    return pl.pallas_call(
        finish_kernel,
        grid=(NT // PER,),
        out_shape=(shape(rows, cols), shape(rows, R), shape(*own), shape(*own)),
        in_specs=[vmem] * 3,
        out_specs=(pl.BlockSpec((rows, PER * W), lambda i: (0, i)), whole(rows, R), whole(*own), whole(*own)),
        compiler_params=pltpu.CompilerParams(vmem_limit_bytes=12 * 1024 * 1024),
    )(nb, low.reshape(NT, R, W), moved)


def solution(mesh):
    in_specs = (P("fsdp", "rep"), P("fsdp", None), P(), P("fsdp", "rep"), P("fsdp", "rep"))
    out_specs = (P("fsdp", "rep"), P("fsdp", None), P("fsdp", "rep"), P("fsdp", "rep"))
    return jax.shard_map(
        per_device, mesh=mesh, in_specs=in_specs, out_specs=out_specs, check_vma=False
    )
```

```python
import jax
import jax.numpy as jnp
from jax import lax
from jax.experimental import pallas as pl
from jax.experimental.pallas import tpu as pltpu
from jax.sharding import PartitionSpec as P

MESH = pl.DeviceIdType.MESH
HIGH = lax.Precision.HIGHEST
F32 = jnp.float32
BF16 = jnp.bfloat16
NY, NZ, NR = 4, 8, 8
NF = NY * NZ
OZ = 7
NT = NY * OZ
R = 256
W = 128
CUT = 96
VMEM_LIMIT = 28 * 1024 * 1024
LO, HI = slice(0, CUT), slice(CUT, R)

NAMES = (
    [f"am{s}{j}" for s in range(4) for j in range(4)]
    + [f"an{s}{j}" for s in range(3) for j in range(4)]
    + ["hm00", "hm10", "hn00"]
    + [f"bm{s}{j}" for s in range(2) for j in range(8)]
    + [f"bn0{j}" for j in range(8)]
    + [f"jm{s}0" for s in range(4)]
    + [f"jn{s}0" for s in range(3)]
)
INDEX = {name: i for i, name in enumerate(NAMES)}
SCATTER_ORDER = (
    "bm00", "am00", "an00", "bn00", "am01", "bm01", "an01", "am02", "bn01", "an02", "bm02", "am03", "an03", "bn02",
    "cz00", "am10", "bm03", "an10", "am11", "bn03", "an11", "ka00", "am12", "bm10", "an12", "bm11", "am13", "bm12",
    "an13", "am20", "bm04", "an20", "am21", "bn04", "an21", "bm05", "am22", "bn05", "jm00", "cy00", "bm06", "an22",
    "am23", "bn06", "kb00", "jn00", "bm07", "an23", "bn07", "am30", "am31", "bm13", "am32", "bm14", "jm10", "bm15",
    "am33", "bm16", "bm17", "jn10", "gx00", "hm00", "jm20", "hn00", "kr00", "jn20", "hm10", "jm30",
)
GATHER_ORDER = (
    "hm00", "jm00", "hn00", "jn00", "bm00", "am00", "an00", "bn00", "am01", "hm10", "an01", "bm01", "jm10", "bn01",
    "am02", "an02", "bm05", "jn10", "bn05", "am10", "an10", "bm10", "am11", "bm11", "am03", "an03", "bm02", "an11",
    "bn02", "jm20", "am12", "bm15", "an12", "bm06", "jn20", "bn06", "am20", "an20", "bm12", "am21", "am13", "bm03",
    "an13", "bn03", "an21", "jm30", "am22", "bm16", "bm07", "bn07", "an22", "bm13", "am30", "am31", "bm04", "am23",
    "an23", "bn04", "am32", "bm17", "am33", "bm14",
)
SCATTER_Y = (2, 1, -1, 0)
SCATTER_Z = (4, 3, -3, 2, -2, 1, -1, 0)
GATHER_Y = (0, -1, 1, -2)
GATHER_Z = (0, -1, -2, -3, -4, 1, 2, 3)


def dot(a, b):
    return jnp.dot(a, b, precision=HIGH, preferred_element_type=F32)


def halves(x):
    top = x.astype(BF16)
    return top, (x - top.astype(F32)).astype(BF16)


def dot3(a, b):
    (ah, al), (bh, bl) = a, b
    one = lambda p, q: jnp.dot(p, q, preferred_element_type=F32)
    return one(ah, bh) + (one(ah, bl) + one(al, bh))


def copy_to(src, dst, ssem, rsem, dev):
    return pltpu.make_async_remote_copy(
        src_ref=src, dst_ref=dst, send_sem=ssem, recv_sem=rsem, device_id=dev, device_id_type=MESH
    )


def columns(row):
    return jnp.transpose(jnp.broadcast_to(row, (W, row.shape[1])))


def scatter_sends():
    need = {}
    for s in range(4):
        need[f"jm{s}0"] = [f"bm1{(0, 1, 3, 5)[s]}", f"bn0{(0, 1, 3, 5)[s]}"] + ([f"jm{s - 1}0"] if s else [])
    for s in range(3):
        need[f"jn{s}0"] = [f"bm1{(2, 4, 6)[s]}", f"bn0{(2, 4, 6)[s]}"] + ([f"jn{s - 1}0"] if s else [])
    need["hm00"] = ["am30", "an20"]
    need["hm10"] = ["am31", "an21", "hm00"]
    need["hn00"] = ["am32", "an22"]
    for j in range(8):
        for s in range(2):
            need[f"bm{s}{j}"] = [f"bm{s - 1}{j}"] if s else [f"P{j}"] + (["cz00"] if j >= 4 else [])
        need[f"bn0{j}"] = [f"P{j}"] + (["cz00"] if j >= 4 else [])
        if j < 4:
            for s in range(4):
                need[f"am{s}{j}"] = [f"am{s - 1}{j}"] if s else ["P0"]
            for s in range(3):
                need[f"an{s}{j}"] = [f"an{s - 1}{j}"] if s else ["P2"]
    return need


def gather_sends():
    need = {"hm00": [], "hn00": [], "hm10": ["hm00"]}
    for s in range(4):
        need[f"jm{s}0"] = [f"jm{s - 1}0"] if s else []
    for s in range(3):
        need[f"jn{s}0"] = [f"jn{s - 1}0"] if s else []
    first = ([], ["hm00"], ["hn00"], ["hm10"])
    for j in range(4):
        for s in range(4):
            need[f"am{s}{j}"] = [f"am{s - 1}{j}"] if s else first[j]
        for s in range(3):
            need[f"an{s}{j}"] = [f"an{s - 1}{j}"] if s else first[j]
    for j in range(8):
        here = [] if j == 0 else [f"jm{j - 1}0" if j < 5 else f"jn{j - 5}0"]
        need[f"bm0{j}"] = here
        need[f"bn0{j}"] = here
        need[f"bm1{j}"] = [f"bm0{j}"]
    return need


class Flow:
    def __init__(self, need, start):
        self.need, self.start, self.done, self.issued = need, start, set(), []

    def issue(self):
        for name, wants in self.need.items():
            if name not in self.issued and self.done.issuperset(wants):
                self.issued.append(name)
                self.start(name)

    def finished(self, name):
        self.done.add(name)
        self.issue()


def kernel(
    grad_in, basis_in, direction_in, first_in, second_in,
    update, new_basis, first_out, second_out,
    grad, basis, direction, first, second, part, low, left_h, left_l, rows_out, sa, sh, sb, sj, csrc, cz, call, gs, hs, vsrc, vs, ps, ss, ka, ksum, kb, kr, kc, kd, msrc, mown, fown,
    bulk_s, bulk_r, small_s, small_r, local_sem,
):
    f = lax.axis_index("fsdp")
    r = lax.axis_index("rep")
    y, z = f // NZ, f % NZ
    flip = r % 2
    owner = z != OZ
    tile = y * OZ + z

    def yadd(k):
        return (y + k - 2 * k * flip + 16) % NY

    def zadd(k):
        return (z + k - 2 * k * flip + 16) % NZ

    def at_y(yy):
        return {"fsdp": yy * NZ + z}

    def at_z(zz):
        return {"fsdp": y * NZ + zz}

    loads = [
        pltpu.make_async_copy(src, dst, local_sem.at[i])
        for i, (src, dst) in enumerate(
            ((direction_in, direction), (basis_in, basis), (first_in, first), (second_in, second))
        )
    ]
    slab = OZ * W
    loads += [
        pltpu.make_async_copy(
            grad_in.at[:, slab * i : slab * (i + 1)], grad.at[:, slab * i : slab * (i + 1)], local_sem.at[4 + i]
        )
        for i in range(NY)
    ]
    for i in (0, 1, 4, 5, 6, 7, 2, 3):
        loads[i].start()

    barrier = pltpu.get_barrier_semaphore()

    def greet_f(i, c):
        pl.semaphore_signal(barrier, inc=1, device_id={"fsdp": (f + i) % NF}, device_id_type=MESH)
        return c

    def greet_r(i, c):
        pl.semaphore_signal(barrier, inc=1, device_id={"rep": (r + i) % NR}, device_id_type=MESH)
        return c

    lax.fori_loop(1, NF, greet_f, 0)
    lax.fori_loop(1, NR, greet_r, 0)

    loads[0].wait()
    loads[1].wait()
    d = direction[...]
    unit = d / jnp.sqrt(jnp.sum(d * d, axis=1, keepdims=True) + 1e-06)
    tcol = jnp.sum(basis[...] * unit, axis=1, keepdims=True)
    twide = jnp.broadcast_to(tcol, (R, W))
    for k in range(NT):
        if k % OZ == 0:
            loads[4 + k // OZ].wait()
        csrc[k] = jnp.sum(twide * grad[:, W * k : W * k + W], axis=0, keepdims=True)

    bt = jnp.transpose(basis[...])
    bth, btl = halves(bt)

    def part_pair(y0, y1, zz):
        cols = lambda yy: pl.ds(pl.multiple_of((yy * OZ + zz) * W, W), W)

        @pl.when(zz != OZ)
        def _():
            block = dot3((bth, btl), halves(jnp.concatenate([grad[:, cols(y0)], grad[:, cols(y1)]], axis=1)))
            part[y0, zz] = block[:, 0:W]
            part[y1, zz] = block[:, W:]

    def part_column(k):
        def go(i, c):
            part_pair(yadd(2 - i), yadd(i - 1), zadd(k))
            return c

        lax.fori_loop(0, 2, go, 0)

    pl.semaphore_wait(barrier, NF - 1 + NR - 1)

    def wait_all(ref, sem):
        pltpu.make_async_copy(ref, ref, sem).wait()

    def peers(kind):
        return {
            "y": (NY, y, at_y),
            "z": (NZ, z, at_z),
            "f": (NF, f, lambda q: {"fsdp": q}),
            "r": (NR, r, lambda q: {"rep": q}),
        }[kind]

    count = [0]

    def swap(kind, slots, src=None):
        n, me, dev = peers(kind)
        ssem, rsem = small_s.at[count[0]], small_r.at[count[0]]
        count[0] += 1

        def start():
            def go(i, c):
                p = (me + i) % n
                source = slots.at[me] if src is None else src(p)
                copy_to(source, slots.at[me], ssem, rsem, dev(p)).start()
                return c

            lax.fori_loop(1, n, go, 0)

        others = slots.at[pl.ds(0, n - 1)]
        return start, lambda: wait_all(others, rsem), lambda: wait_all(others, ssem)

    g_x = swap("r", gs)
    h_x = swap("f", hs)
    p_x = swap("r", ps)
    s_x = swap("f", ss)
    k_a = swap("y", ka, src=lambda p: ka.at[NY + p])
    k_b = swap("z", kb, src=lambda p: ksum.at[p])
    k_r = swap("z", kr)
    k_c = swap("y", kc)
    k_d = swap("r", kd)
    v_s, v_r, m_s, m_r, o_s, o_r, c_s, c_r, d_s, d_r = (x.at[9 + i] for i in range(5) for x in (small_s, small_r))

    def owners_but_me(ref, sem):
        pl.when(owner)(lambda: wait_all(ref.at[pl.ds(0, NT - 1)], sem))
        pl.when(z == OZ)(lambda: wait_all(ref.at[pl.ds(0, NT)], sem))

    def spot(yy, zz, kind):
        return part.at[yy, zz, LO if kind in "ah" else HI, :]

    def slot_of(name):
        i = INDEX[name]
        for ref in (sa, sh, sb, sj):
            if i < ref.shape[0]:
                return ref.at[i]
            i -= ref.shape[0]

    def scatter_route(name):
        kind, way, s, j = name[0], name[1], int(name[2]), int(name[3])
        main = way == "m"
        if kind == "a":
            yy = yadd(SCATTER_Y[j])
            zs, zr = (zadd(4 - s), zadd(3 - s)) if main else (zadd(s - 3), zadd(s - 2))
            return (yy, zs), (yy, zr), at_z(zadd(1 if main else -1)), zs, zr
        if kind == "j":
            zs, zr = (zadd(4 - s), zadd(3 - s)) if main else (zadd(s - 3), zadd(s - 2))
            return (y, zs), (y, zr), at_z(zadd(1 if main else -1)), zs, zr
        zz = z if kind == "h" else zadd(SCATTER_Z[j])
        ys, yr = (yadd(2 - s), yadd(1 - s)) if main else (yadd(-1), y)
        return (ys, zz), (yr, zz), at_y(yadd(1 if main else -1)), zz, zz

    def scatter_copy(name, to_send):
        leave, arrive, dev, zs, zr = scatter_route(name)
        i = INDEX[name]
        where = leave if to_send else arrive
        one = lambda: copy_to(spot(*where, name[0]), slot_of(name), bulk_s.at[i], bulk_r.at[i], dev)
        return one, (zs if to_send else zr) != OZ, spot(*arrive, name[0])

    def scatter_start(name):
        one, there, _ = scatter_copy(name, True)
        pl.when(there)(lambda: one().start())

    def scatter_take(name):
        one, there, ref = scatter_copy(name, False)

        @pl.when(there)
        def _():
            one().wait_recv()
            ref[...] += slot_of(name)[...]

    values = {}

    def c_start(i, c):
        p = (f + i) % NF
        t = (p // NZ) * OZ + p % NZ
        pl.when(p % NZ != OZ)(lambda: copy_to(csrc.at[t], cz.at[f], c_s, c_r, {"fsdp": p}).start())
        return c

    def d_start(i, c):
        copy_to(call.at[tile], call.at[tile], d_s, d_r, {"fsdp": (f + i) % NF}).start()
        return c

    def on_cz():
        @pl.when(owner)
        def _():
            wait_all(cz.at[pl.ds(0, NF - 1)], c_r)
            cz[f] = csrc[tile]
            call[tile] = jnp.sum(cz[...], axis=0)
            lax.fori_loop(1, NF, d_start, 0)

    def on_cy():
        owners_but_me(call, d_r)
        acc = grad[:, 0:W] * call[0]
        for k in range(1, NT):
            acc += grad[:, W * k : W * k + W] * call[k]
        gs[r] = jnp.sum(jnp.transpose(acc), axis=0, keepdims=True)
        g_x[0]()

    def v_start(i, c):
        p = (f + i) % NF
        t = (p // NZ) * OZ + p % NZ
        pl.when(p % NZ != OZ)(lambda: copy_to(vsrc.at[t], vs.at[f], v_s, v_r, {"fsdp": p}).start())
        return c

    def on_gx():
        g_x[1]()
        gcol = columns(jnp.sum(gs[...], axis=0))
        values["g"] = gcol
        hs[f] = jnp.sum(jnp.concatenate([gcol, gcol], axis=1) * basis[...], axis=0, keepdims=True)
        h_x[0]()
        for k in range(NT):
            vsrc[k] = jnp.sum(gcol * grad[:, W * k : W * k + W], axis=0, keepdims=True)
        lax.fori_loop(1, NF, v_start, 0)

    def on_hx():
        h_x[1]()
        hrow = jnp.sum(hs[...], axis=0)
        lifted = values["g"][:, 0:1] - jnp.sum(basis[...] * hrow, axis=1, keepdims=True)
        values["h"], values["lifted"] = hrow, lifted
        values["sig"] = jnp.sum(lifted * lifted, axis=0, keepdims=True)

    def on_ka():
        ka[y] = ka[NY + y]
        k_a[1]()
        rows = (ka[0] + ka[1]) + (ka[2] + ka[3])
        for i in range(NZ):
            ksum[i] = rows[i : i + 1, :]
        k_b[0]()

    def on_kb():
        kb[z] = ksum[z]
        k_b[1]()
        kr[z] = jnp.sum(kb[...], axis=0)
        k_r[0]()

    def on_kr():
        k_r[1]()
        for i in range(NZ):
            kc[y, i : i + 1, :] = kr[i]
        k_c[0]()

    def on_kc():
        k_c[1]()
        for i in range(NY):
            kd[r, 8 * i : 8 * i + 8, :] = kc[i]
        k_d[0]()

    def m_start(i, c):
        p = (f + i) % NF
        t = (p // NZ) * OZ + p % NZ
        rows = pl.ds(pl.multiple_of(8 * f, 8), 8)
        pl.when(p % NZ != OZ)(lambda: copy_to(msrc.at[t], mown.at[:, rows, :], m_s, m_r, {"fsdp": p}).start())
        return c

    chain = {
        "cz00": on_cz, "cy00": on_cy, "gx00": on_gx,
        "ka00": on_ka, "kb00": on_kb, "kr00": on_kr,
    }

    lax.fori_loop(1, NF, c_start, 0)
    scatter = Flow(scatter_sends(), scatter_start)
    part_column(4)
    scatter.finished("P0")
    part_column(-3)
    scatter.finished("P2")
    for j in (1, 3, 4, 5, 6, 7):
        part_pair(yadd(2), yadd(-1), zadd(SCATTER_Z[j]))
        scatter.finished(f"P{j}")

    def part_rest(i, c):
        part_pair(yadd(1), y, zadd(3 - i))
        return c

    lax.fori_loop(0, 6, part_rest, 0)

    gram = dot(bt, basis[...])
    fown[0] = gram[:, 0:W]
    fown[1] = gram[:, W:]
    for i in range(NY):
        rows = pl.ds(pl.multiple_of(32 * r + 8 * i, 8), 8)
        ka[NY + i, :, 0:W] = fown[0, rows, :]
        ka[NY + i, :, W:] = fown[1, rows, :]
    k_a[0]()

    loads[2].wait()
    loads[3].wait()
    for k in range(NT):
        msrc[k, 0] = first[:, W * k : W * k + W]
        msrc[k, 1] = second[:, W * k : W * k + W]

    def spread(step, size, fn):
        low_end, high_end = 1 + step * size, min(1 + (step + 1) * size, NF)
        if step >= 0 and low_end < high_end:
            lax.fori_loop(low_end, high_end, fn, 0)

    for at, name in enumerate(SCATTER_ORDER):
        if name in chain:
            chain[name]()
        else:
            scatter_take(name)
        scatter.finished(name)

    @pl.when(owner)
    def _():
        own = part[y, z]
        ps[r] = jnp.broadcast_to(jnp.sum(jnp.sum(own * own, axis=0, keepdims=True), axis=1, keepdims=True), (1, W))

    @pl.when(z == OZ)
    def _():
        ps[r] = jnp.zeros((1, W), F32)

    p_x[0]()
    on_kc()
    lax.fori_loop(1, NF, m_start, 0)
    on_hx()

    p_x[1]()
    prow = jnp.sum(ps[...], axis=0)
    lane = lax.broadcasted_iota(jnp.int32, (1, W), 1)
    ss[f] = jnp.where(lane < W // 2, jnp.broadcast_to(values["sig"], (1, W)), prow)
    s_x[0]()
    k_d[1]()

    for x in (g_x, h_x, k_a, k_b, k_r, k_c, k_d):
        x[2]()
    for name in scatter.issued:
        one, there = scatter_copy(name, True)[:2]
        pl.when(there)(lambda one=one: one().wait_send())
    owners_but_me(csrc, c_s)
    pl.when(owner)(lambda: wait_all(cz.at[pl.ds(0, NF - 1)], d_s))
    owners_but_me(vsrc, v_s)
    owners_but_me(msrc, m_s)

    @pl.when(owner)
    def _():
        wait_all(vs.at[pl.ds(0, NF - 1)], v_r)
        wait_all(mown.at[:, pl.ds(0, R - 8), :], m_r)
        mown[:, pl.ds(pl.multiple_of(8 * f, 8), 8), :] = msrc[tile]
        vs[f] = vsrc[tile]

    s_x[1]()
    norms = jnp.sum(ss[...], axis=0)
    opposite = 0.2 * jnp.sqrt(norms[:, 0:1] + 1e-06)
    adjacent = jnp.sqrt(norms[:, W - 1 : W] + 1e-06)
    top = jnp.maximum(opposite, adjacent)
    opp, adj = opposite / top, adjacent / top
    hyp = jnp.sqrt(opp * opp + adj * adj)
    cos_less = -(opp * opp) / (hyp * (hyp + adj))
    sin_over = (opp / hyp) / (5.0 * opposite)
    hrow, lifted = values["h"], values["lifted"]

    @pl.when(owner)
    def _():
        ucol = columns(unit)
        ucol2 = jnp.concatenate([ucol, ucol], axis=1)
        k0 = kd[...].reshape(R, R)
        ku = jnp.sum(ucol2 * k0, axis=0, keepdims=True)
        hcol = columns(hrow)
        hcol2 = jnp.concatenate([hcol, hcol], axis=1)
        kh = jnp.sum(hcol2 * k0, axis=0, keepdims=True)
        beta = cos_less * ku + sin_over * (hrow - kh)
        rot = k0 + ucol2 * beta
        own = part[y, z]
        hp = jnp.sum(hcol * own, axis=0, keepdims=True)
        cown = call[tile]
        wrow = cos_less * cown + sin_over * (jnp.sum(vs[...], axis=0) - hp)
        proj = own + ucol * wrow
        fo = 0.9 * dot(rot, mown[0]) + 0.1 * proj
        so = 0.99 * dot(rot * rot, mown[1]) + 0.01 * proj * proj
        fown[1] = so
        low[y, z] = fo / (jnp.sqrt(so) + 1e-08)

    def gather_route(name):
        kind, way, s, j = name[0], name[1], int(name[2]), int(name[3])
        main = way == "m"
        if kind in "aj":
            yy = yadd(GATHER_Y[j]) if kind == "a" else y
            zs, zr = (zadd(-s), zadd(-1 - s)) if main else (zadd(s), zadd(1 + s))
            return (yy, zs), (yy, zr), at_z(zadd(1 if main else -1))
        zz = z if kind == "h" else zadd(GATHER_Z[j])
        ys, yr = (yadd(-s), yadd(-1 - s)) if main else (y, yadd(1))
        return (ys, zz), (yr, zz), at_y(yadd(1 if main else -1))

    def gather_copy(name, to_send):
        leave, arrive, dev = gather_route(name)
        i = INDEX[name]
        rows = LO if name[0] in "ah" else HI
        yy, zz = leave if to_send else arrive

        def one():
            dst = low.at[yy, zz, rows, :]
            return copy_to(dst, dst, bulk_s.at[i], bulk_r.at[i], dev)

        return one, zz != OZ

    def gather_start(name):
        one, there = gather_copy(name, True)
        pl.when(there)(lambda: one().start())

    def gather_take(name):
        one, there = gather_copy(name, False)
        pl.when(there)(lambda: one().wait_recv())

    gather = Flow(gather_sends(), gather_start)
    gather.issue()

    own_rows = pl.ds(pl.multiple_of(8 * f, 8), 8)
    nb = basis[...] + (cos_less * tcol + sin_over * lifted) * unit
    new_basis[...] = nb
    left_h[...], left_l[...] = halves(nb)

    @pl.when(owner)
    def _():
        rows_out[tile] = fown[1, own_rows, :]

    columns_need = {0: {"hm00", "hn00", "hm10", "bm00", "bn00", "bm10"}}
    for s in range(4):
        columns_need[-1 - s] = {f"am{s}{j}" for j in range(4)} | {f"jm{s}0", f"bm0{s + 1}", f"bn0{s + 1}", f"bm1{s + 1}"}
    for s in range(3):
        columns_need[1 + s] = {f"an{s}{j}" for j in range(4)} | {f"jn{s}0", f"bm0{s + 5}", f"bn0{s + 5}", f"bm1{s + 5}"}
    ready = []

    def whole_columns():
        for k in [k for k, names in columns_need.items() if gather.done.issuperset(names)]:
            del columns_need[k]
            ready.extend(((k, 0), (k, 2)))

    def update_next():
        if not ready:
            return
        k, yy = ready.pop(0)
        zz = zadd(k)

        @pl.when(zz != OZ)
        def _():
            block = dot3((left_h[...], left_l[...]), halves(jnp.concatenate([low[yy, zz], low[yy + 1, zz]], axis=1)))
            update[yy, zz] = block[:, 0:W]
            update[yy + 1, zz] = block[:, W:]

    def o_start(i, c):
        p = (f + i) % NF
        rows = pl.ds(pl.multiple_of(8 * p, 8), 8)
        copy_to(fown.at[1, rows, :], rows_out.at[tile], o_s, o_r, {"fsdp": p}).start()
        return c

    for at, name in enumerate(GATHER_ORDER):
        gather_take(name)
        gather.finished(name)
        whole_columns()
        update_next()
        if at >= 10:
            pl.when(owner)(lambda: spread(at - 10, 1, o_start))

    while ready:
        update_next()
    owners_but_me(rows_out, o_r)
    for k in range(NT):
        mixed = rows_out[k]
        second_out[:, W * k : W * k + W] = mixed
        first_out[:, W * k : W * k + W] = low[k // OZ, k % OZ, own_rows, :] * (jnp.sqrt(mixed) + 1e-08)

    p_x[2]()
    s_x[2]()
    for name in gather.issued:
        one, there = gather_copy(name, True)
        pl.when(there)(lambda one=one: one().wait_send())

    @pl.when(owner)
    def _():
        wait_all(fown.at[1, pl.ds(0, R - 8), :], o_s)


def copy_out(tiles, nb, first, second, update, new_basis, first_out, second_out, sems):
    for k in range(NT):
        pltpu.make_async_copy(tiles.at[k // OZ, k % OZ], update.at[:, W * k : W * k + W], sems.at[0]).start()
    rest = [
        pltpu.make_async_copy(src, dst, sems.at[1 + i])
        for i, (src, dst) in enumerate(((nb, new_basis), (first, first_out), (second, second_out)))
    ]
    for one in rest:
        one.start()
    pltpu.make_async_copy(tiles, tiles, sems.at[0]).wait()
    for one in rest:
        one.wait()


def per_device(gradient, basis, direction, first_moment, second_moment):
    vmem = pl.BlockSpec(memory_space=pltpu.VMEM)
    anywhere = pl.BlockSpec(memory_space=pl.ANY)
    dma = pltpu.SemaphoreType.DMA
    v = lambda *shape: pltpu.VMEM(shape, F32)
    shape = lambda *s: jax.ShapeDtypeStruct(s, F32)
    rows, cols = gradient.shape
    own = first_moment.shape
    scratch = [
        v(rows, cols), v(rows, R), v(1, R), v(*own), v(*own),
        v(NY, OZ, R, W), v(NY, OZ, R, W),
        pltpu.VMEM((rows, R), BF16), pltpu.VMEM((rows, R), BF16), v(NT, 8, W),
        v(28, CUT, W), v(3, CUT, W), v(24, R - CUT, W), v(7, R - CUT, W),
        v(NT, 1, W), v(NF, 1, W), v(NT, 1, W), v(NR, 1, R), v(NF, 1, R),
        v(NT, 1, W), v(NF, 1, W), v(NR, 1, W), v(NF, 1, W),
        v(2 * NY, 8, R), v(NZ, 1, R), v(NZ, 1, R), v(NZ, 1, R), v(NY, 8, R), v(NR, 32, R),
        v(NT, 2, 8, W), v(2, R, W), v(2, R, W),
    ]
    sems = [len(NAMES), len(NAMES), 14, 14, 10]
    arrays = (gradient, basis, direction.reshape(1, R), first_moment, second_moment)
    moved = pl.pallas_call(
        kernel,
        out_shape=(shape(NY, OZ, R, W), shape(rows, R), shape(*own), shape(*own)),
        in_specs=[pl.BlockSpec(memory_space=pltpu.HBM)] * 5,
        out_specs=(vmem,) * 4,
        scratch_shapes=scratch + [dma((k,)) for k in sems],
        compiler_params=pltpu.CompilerParams(
            collective_id=0, has_side_effects=True, vmem_limit_bytes=VMEM_LIMIT
        ),
    )(*(pltpu.with_memory_space_constraint(x, pltpu.HBM) for x in arrays))
    return pl.pallas_call(
        copy_out,
        out_shape=(shape(rows, cols), shape(rows, R), shape(*own), shape(*own)),
        in_specs=[vmem] * 4,
        out_specs=(anywhere,) * 4,
        scratch_shapes=[dma((4,))],
        compiler_params=pltpu.CompilerParams(vmem_limit_bytes=12 * 1024 * 1024),
    )(*moved)


def solution(mesh):
    in_specs = (P("fsdp", "rep"), P("fsdp", None), P(), P("fsdp", "rep"), P("fsdp", "rep"))
    out_specs = (P("fsdp", "rep"), P("fsdp", None), P("fsdp", "rep"), P("fsdp", "rep"))
    return jax.shard_map(
        per_device, mesh=mesh, in_specs=in_specs, out_specs=out_specs, check_vma=False
    )
```

```python
import jax
import jax.numpy as jnp
from jax import lax
from jax.experimental import pallas as pl
from jax.experimental.pallas import tpu as pltpu
from jax.sharding import PartitionSpec as P

MESH = pl.DeviceIdType.MESH
HIGH = lax.Precision.HIGHEST
F32 = jnp.float32
BF16 = jnp.bfloat16
NY, NZ, NR = 4, 8, 8
NF = NY * NZ
OZ = 7
NT = NY * OZ
R = 256
W = 128
CUT = 96
VMEM_LIMIT = 28 * 1024 * 1024
LO, HI = slice(0, CUT), slice(CUT, R)

NAMES = (
    [f"am{s}{j}" for s in range(4) for j in range(4)]
    + [f"an{s}{j}" for s in range(3) for j in range(4)]
    + ["hm00", "hm10", "hn00"]
    + [f"bm{s}{j}" for s in range(2) for j in range(8)]
    + [f"bn0{j}" for j in range(8)]
    + [f"jm{s}0" for s in range(4)]
    + [f"jn{s}0" for s in range(3)]
)
INDEX = {name: i for i, name in enumerate(NAMES)}
SCATTER_PLAN = (
    "P0", ">bm00", ">am00", ">bn00", ">am01", ">am02", ">am03", "P2", ">bm02", ">an00", ">bn02", ">an01", "P1",
    "P3", ">an02", "P4", ">bm01", ">an03", "P5", "P6", ">bn01", "P7", ">bm03", ">bm04", "*", "am00",
    ">am10", ">bn03", "bm00", "am01", ">am11", "am02", ">am12", "bn00", "am03", ">bm10", ">am13", "bm02", "an00",
    ">an10", "an01", ">an11", "bn02", "an02", ">an12", "an03", ">bm12", "bm01", "bn01", "cz00", ">an13", "bm03",
    "am10", ">bm11", ">am20", "am11", ">am21", "bm04", "am12", ">bm13", ">am22", "am13", ">am23", "bn03", ">bm14",
    "an10", ">an20", "ka00", "an11", ">bn04", ">an21", "bm10", "an12", ">jm00", "bm12", ">bm05", "an13", "am20",
    ">jn00", "am21", ">bm06", "bm11", ">am30", "am22", ">bn05", "bm13", ">am31", "am23", "an20", ">bn06", ">am32",
    "bm14", ">an22", "an21", ">bm07", ">am33", "bn04", "jm00", ">jm10", ">bn07", "bm05", "jn00", ">bm15", ">jn10",
    "cy00", ">an23", "bm06", ">bm16", "am30", "am31", "bn05", "kb00", ">hm00", "am32", "bn06", "an22", ">hn00",
    "am33", "bm07", ">bm17", "jm10", ">jm20", "bn07", "jn10", "bm15", "an23", "bm16", ">jn20", "hm00", ">hm10",
    "jm20", ">jm30", "hn00", "bm17", "jn20", "kr00", "gx00", "hm10", "jm30",
)
GATHER_PLAN = (
    ">jm00", ">hm00", ">jn00", ">hn00", ">am00", ">an00", ">bm00", ">bn00", "hm00", ">hm10", ">am01", ">an01", "jm00",
    ">jm10", ">bm01", ">bn01", "hn00", ">am02", ">an02", "jn00", ">jn10", ">bm05", ">bn05", "bm00", "am00", "an00",
    ">am10", ">an10", ">bm10", "bn00", "am01", ">am11", "hm10", "an01", "bm01", ">am03", ">bm11", "jm10", ">jm20",
    ">bm02", "bn01", "am02", "an02", ">am12", ">bn02", "bm05", "jn10", ">jn20", ">bm06", "bn05", "am10", ">an03",
    ">bm15", "an10", "bm10", "am11", "bm11", ">am20", ">am21", ">bn06", "am03", "bm02", ">am13", ">bm12", "jm20",
    "bn02", ">jm30", ">bm03", "am12", ">bn03", ">an20", "bm06", "jn20", "an03", ">bm07", ">an11", ">am22", "bm15",
    "am20", ">an12", ">bm16", "bn06", "am21", ">an13", ">bn07", "am13", ">am23", "bm12", "bm03", ">bm13", ">am30",
    "jm30", ">bm04", ">am31", "an20", "bn03", "an11", ">bn04", ">an21", "bm07", ">bm17", "am22", ">am32", "an12",
    ">an22", "bm16", "an13", ">an23", "bn07", "am23", ">am33", "am30", "bm13", "am31", "bm04", ">bm14", "an21",
    "am32", "bn04", "an22", "an23", "bm17", "am33", "bm14",
)
SCATTER_Y = (2, 1, -1, 0)
SCATTER_Z = (4, 3, -3, 2, -2, 1, -1, 0)
GATHER_Y = (0, -1, 1, -2)
GATHER_Z = (0, -1, -2, -3, -4, 1, 2, 3)


def dot(a, b):
    return jnp.dot(a, b, precision=HIGH, preferred_element_type=F32)


def halves(x):
    top = x.astype(BF16)
    return top, (x - top.astype(F32)).astype(BF16)


def dot3(a, b):
    (ah, al), (bh, bl) = a, b
    one = lambda p, q: jnp.dot(p, q, preferred_element_type=F32)
    return one(ah, bh) + (one(ah, bl) + one(al, bh))


def copy_to(src, dst, ssem, rsem, dev):
    return pltpu.make_async_remote_copy(
        src_ref=src, dst_ref=dst, send_sem=ssem, recv_sem=rsem, device_id=dev, device_id_type=MESH
    )


def columns(row):
    return jnp.transpose(jnp.broadcast_to(row, (W, row.shape[1])))


def kernel(
    grad_in, basis_in, direction_in, first_in, second_in,
    update, new_basis, first_out, second_out,
    grad, basis, direction, first, second, part, low, left_h, left_l, rows_out, sa, sh, sb, sj, csrc, cz, call, gs, hs, vsrc, vs, ps, ss, ka, ksum, kb, kr, kc, kd, msrc, mown, fown,
    bulk_s, bulk_r, small_s, small_r, local_sem,
):
    f = lax.axis_index("fsdp")
    r = lax.axis_index("rep")
    y, z = f // NZ, f % NZ
    flip = r % 2
    owner = z != OZ
    tile = y * OZ + z

    def yadd(k):
        return (y + k - 2 * k * flip + 16) % NY

    def zadd(k):
        return (z + k - 2 * k * flip + 16) % NZ

    def at_y(yy):
        return {"fsdp": yy * NZ + z}

    def at_z(zz):
        return {"fsdp": y * NZ + zz}

    loads = [
        pltpu.make_async_copy(src, dst, local_sem.at[i])
        for i, (src, dst) in enumerate(
            ((direction_in, direction), (basis_in, basis), (first_in, first), (second_in, second))
        )
    ]
    slab = OZ * W
    loads += [
        pltpu.make_async_copy(
            grad_in.at[:, slab * i : slab * (i + 1)], grad.at[:, slab * i : slab * (i + 1)], local_sem.at[4 + i]
        )
        for i in range(NY)
    ]
    for i in (0, 1, 4, 5, 6, 7, 2, 3):
        loads[i].start()

    barrier = pltpu.get_barrier_semaphore()

    def greet_f(i, c):
        pl.semaphore_signal(barrier, inc=1, device_id={"fsdp": (f + i) % NF}, device_id_type=MESH)
        return c

    def greet_r(i, c):
        pl.semaphore_signal(barrier, inc=1, device_id={"rep": (r + i) % NR}, device_id_type=MESH)
        return c

    lax.fori_loop(1, NF, greet_f, 0)
    lax.fori_loop(1, NR, greet_r, 0)

    loads[0].wait()
    loads[1].wait()
    d = direction[...]
    unit = d / jnp.sqrt(jnp.sum(d * d, axis=1, keepdims=True) + 1e-06)
    tcol = jnp.sum(basis[...] * unit, axis=1, keepdims=True)
    twide = jnp.broadcast_to(tcol, (R, W))
    for k in range(NT):
        if k % OZ == 0:
            loads[4 + k // OZ].wait()
        csrc[k] = jnp.sum(twide * grad[:, W * k : W * k + W], axis=0, keepdims=True)

    bt = jnp.transpose(basis[...])
    bth, btl = halves(bt)

    def part_pair(y0, y1, zz):
        cols = lambda yy: pl.ds(pl.multiple_of((yy * OZ + zz) * W, W), W)

        @pl.when(zz != OZ)
        def _():
            block = dot3((bth, btl), halves(jnp.concatenate([grad[:, cols(y0)], grad[:, cols(y1)]], axis=1)))
            part[y0, zz] = block[:, 0:W]
            part[y1, zz] = block[:, W:]

    def part_column(k):
        def go(i, c):
            part_pair(yadd(2 - i), yadd(i - 1), zadd(k))
            return c

        lax.fori_loop(0, 2, go, 0)

    pl.semaphore_wait(barrier, NF - 1 + NR - 1)

    def wait_all(ref, sem):
        pltpu.make_async_copy(ref, ref, sem).wait()

    def peers(kind):
        return {
            "y": (NY, y, at_y),
            "z": (NZ, z, at_z),
            "f": (NF, f, lambda q: {"fsdp": q}),
            "r": (NR, r, lambda q: {"rep": q}),
        }[kind]

    count = [0]

    def swap(kind, slots, src=None):
        n, me, dev = peers(kind)
        ssem, rsem = small_s.at[count[0]], small_r.at[count[0]]
        count[0] += 1

        def start():
            def go(i, c):
                p = (me + i) % n
                source = slots.at[me] if src is None else src(p)
                copy_to(source, slots.at[me], ssem, rsem, dev(p)).start()
                return c

            lax.fori_loop(1, n, go, 0)

        others = slots.at[pl.ds(0, n - 1)]
        return start, lambda: wait_all(others, rsem), lambda: wait_all(others, ssem)

    g_x = swap("r", gs)
    h_x = swap("f", hs)
    p_x = swap("r", ps)
    s_x = swap("f", ss)
    k_a = swap("y", ka, src=lambda p: ka.at[NY + p])
    k_b = swap("z", kb, src=lambda p: ksum.at[p])
    k_r = swap("z", kr)
    k_c = swap("y", kc)
    k_d = swap("r", kd)
    v_s, v_r, m_s, m_r, o_s, o_r, c_s, c_r, d_s, d_r = (x.at[9 + i] for i in range(5) for x in (small_s, small_r))

    def owners_but_me(ref, sem):
        pl.when(owner)(lambda: wait_all(ref.at[pl.ds(0, NT - 1)], sem))
        pl.when(z == OZ)(lambda: wait_all(ref.at[pl.ds(0, NT)], sem))

    def spot(yy, zz, kind):
        return part.at[yy, zz, LO if kind in "ah" else HI, :]

    def slot_of(name):
        i = INDEX[name]
        for ref in (sa, sh, sb, sj):
            if i < ref.shape[0]:
                return ref.at[i]
            i -= ref.shape[0]

    def scatter_route(name):
        kind, way, s, j = name[0], name[1], int(name[2]), int(name[3])
        main = way == "m"
        if kind == "a":
            yy = yadd(SCATTER_Y[j])
            zs, zr = (zadd(4 - s), zadd(3 - s)) if main else (zadd(s - 3), zadd(s - 2))
            return (yy, zs), (yy, zr), at_z(zadd(1 if main else -1)), zs, zr
        if kind == "j":
            zs, zr = (zadd(4 - s), zadd(3 - s)) if main else (zadd(s - 3), zadd(s - 2))
            return (y, zs), (y, zr), at_z(zadd(1 if main else -1)), zs, zr
        zz = z if kind == "h" else zadd(SCATTER_Z[j])
        ys, yr = (yadd(2 - s), yadd(1 - s)) if main else (yadd(-1), y)
        return (ys, zz), (yr, zz), at_y(yadd(1 if main else -1)), zz, zz

    def scatter_copy(name, to_send):
        leave, arrive, dev, zs, zr = scatter_route(name)
        i = INDEX[name]
        where = leave if to_send else arrive
        one = lambda: copy_to(spot(*where, name[0]), slot_of(name), bulk_s.at[i], bulk_r.at[i], dev)
        return one, (zs if to_send else zr) != OZ, spot(*arrive, name[0])

    def scatter_start(name):
        one, there, _ = scatter_copy(name, True)
        pl.when(there)(lambda: one().start())

    def scatter_take(name):
        one, there, ref = scatter_copy(name, False)

        @pl.when(there)
        def _():
            one().wait_recv()
            ref[...] += slot_of(name)[...]

    values = {}

    def c_start(i, c):
        p = (f + i) % NF
        t = (p // NZ) * OZ + p % NZ
        pl.when(p % NZ != OZ)(lambda: copy_to(csrc.at[t], cz.at[f], c_s, c_r, {"fsdp": p}).start())
        return c

    def d_start(i, c):
        copy_to(call.at[tile], call.at[tile], d_s, d_r, {"fsdp": (f + i) % NF}).start()
        return c

    def on_cz():
        @pl.when(owner)
        def _():
            wait_all(cz.at[pl.ds(0, NF - 1)], c_r)
            cz[f] = csrc[tile]
            call[tile] = jnp.sum(cz[...], axis=0)
            lax.fori_loop(1, NF, d_start, 0)

    def on_cy():
        owners_but_me(call, d_r)
        acc = grad[:, 0:W] * call[0]
        for k in range(1, NT):
            acc += grad[:, W * k : W * k + W] * call[k]
        gs[r] = jnp.sum(jnp.transpose(acc), axis=0, keepdims=True)
        g_x[0]()

    def v_start(i, c):
        p = (f + i) % NF
        t = (p // NZ) * OZ + p % NZ
        pl.when(p % NZ != OZ)(lambda: copy_to(vsrc.at[t], vs.at[f], v_s, v_r, {"fsdp": p}).start())
        return c

    def on_gx():
        g_x[1]()
        gcol = columns(jnp.sum(gs[...], axis=0))
        values["g"] = gcol
        hs[f] = jnp.sum(jnp.concatenate([gcol, gcol], axis=1) * basis[...], axis=0, keepdims=True)
        h_x[0]()
        for k in range(NT):
            vsrc[k] = jnp.sum(gcol * grad[:, W * k : W * k + W], axis=0, keepdims=True)
        lax.fori_loop(1, NF, v_start, 0)

    def on_hx():
        h_x[1]()
        hrow = jnp.sum(hs[...], axis=0)
        lifted = values["g"][:, 0:1] - jnp.sum(basis[...] * hrow, axis=1, keepdims=True)
        values["h"], values["lifted"] = hrow, lifted
        values["sig"] = jnp.sum(lifted * lifted, axis=0, keepdims=True)

    def on_ka():
        ka[y] = ka[NY + y]
        k_a[1]()
        rows = (ka[0] + ka[1]) + (ka[2] + ka[3])
        for i in range(NZ):
            ksum[i] = rows[i : i + 1, :]
        k_b[0]()

    def on_kb():
        kb[z] = ksum[z]
        k_b[1]()
        kr[z] = jnp.sum(kb[...], axis=0)
        k_r[0]()

    def on_kr():
        k_r[1]()
        for i in range(NZ):
            kc[y, i : i + 1, :] = kr[i]
        k_c[0]()

    def on_kc():
        k_c[1]()
        for i in range(NY):
            kd[r, 8 * i : 8 * i + 8, :] = kc[i]
        k_d[0]()

    def m_start(i, c):
        p = (f + i) % NF
        t = (p // NZ) * OZ + p % NZ
        rows = pl.ds(pl.multiple_of(8 * f, 8), 8)
        pl.when(p % NZ != OZ)(lambda: copy_to(msrc.at[t], mown.at[:, rows, :], m_s, m_r, {"fsdp": p}).start())
        return c

    chain = {
        "cz00": on_cz, "cy00": on_cy, "gx00": on_gx,
        "ka00": on_ka, "kb00": on_kb, "kr00": on_kr,
    }

    lax.fori_loop(1, NF, c_start, 0)

    def part_rest(i, c):
        part_pair(yadd(1), y, zadd(3 - i))
        return c

    def part_step(j):
        if j in (0, 2):
            part_column(SCATTER_Z[j])
        else:
            part_pair(yadd(2), yadd(-1), zadd(SCATTER_Z[j]))

    def local_rest():
        lax.fori_loop(0, 6, part_rest, 0)
        gram = dot(bt, basis[...])
        fown[0] = gram[:, 0:W]
        fown[1] = gram[:, W:]
        for i in range(NY):
            rows = pl.ds(pl.multiple_of(32 * r + 8 * i, 8), 8)
            ka[NY + i, :, 0:W] = fown[0, rows, :]
            ka[NY + i, :, W:] = fown[1, rows, :]
        k_a[0]()

        loads[2].wait()
        loads[3].wait()
        for k in range(NT):
            msrc[k, 0] = first[:, W * k : W * k + W]
            msrc[k, 1] = second[:, W * k : W * k + W]

    def spread(step, size, fn):
        low_end, high_end = 1 + step * size, min(1 + (step + 1) * size, NF)
        if step >= 0 and low_end < high_end:
            lax.fori_loop(low_end, high_end, fn, 0)

    for name in SCATTER_PLAN:
        if name == "*":
            local_rest()
        elif name[0] == "P":
            part_step(int(name[1]))
        elif name[0] == ">":
            scatter_start(name[1:])
        elif name in chain:
            chain[name]()
        else:
            scatter_take(name)

    @pl.when(owner)
    def _():
        own = part[y, z]
        ps[r] = jnp.broadcast_to(jnp.sum(jnp.sum(own * own, axis=0, keepdims=True), axis=1, keepdims=True), (1, W))

    @pl.when(z == OZ)
    def _():
        ps[r] = jnp.zeros((1, W), F32)

    p_x[0]()
    on_kc()
    lax.fori_loop(1, NF, m_start, 0)
    on_hx()

    p_x[1]()
    prow = jnp.sum(ps[...], axis=0)
    lane = lax.broadcasted_iota(jnp.int32, (1, W), 1)
    ss[f] = jnp.where(lane < W // 2, jnp.broadcast_to(values["sig"], (1, W)), prow)
    s_x[0]()
    k_d[1]()

    for x in (g_x, h_x, k_a, k_b, k_r, k_c, k_d):
        x[2]()
    for name in NAMES:
        one, there = scatter_copy(name, True)[:2]
        pl.when(there)(lambda one=one: one().wait_send())
    owners_but_me(csrc, c_s)
    pl.when(owner)(lambda: wait_all(cz.at[pl.ds(0, NF - 1)], d_s))
    owners_but_me(vsrc, v_s)
    owners_but_me(msrc, m_s)

    @pl.when(owner)
    def _():
        wait_all(vs.at[pl.ds(0, NF - 1)], v_r)
        wait_all(mown.at[:, pl.ds(0, R - 8), :], m_r)
        mown[:, pl.ds(pl.multiple_of(8 * f, 8), 8), :] = msrc[tile]
        vs[f] = vsrc[tile]

    s_x[1]()
    norms = jnp.sum(ss[...], axis=0)
    opposite = 0.2 * jnp.sqrt(norms[:, 0:1] + 1e-06)
    adjacent = jnp.sqrt(norms[:, W - 1 : W] + 1e-06)
    top = jnp.maximum(opposite, adjacent)
    opp, adj = opposite / top, adjacent / top
    hyp = jnp.sqrt(opp * opp + adj * adj)
    cos_less = -(opp * opp) / (hyp * (hyp + adj))
    sin_over = (opp / hyp) / (5.0 * opposite)
    hrow, lifted = values["h"], values["lifted"]

    @pl.when(owner)
    def _():
        ucol = columns(unit)
        ucol2 = jnp.concatenate([ucol, ucol], axis=1)
        k0 = kd[...].reshape(R, R)
        ku = jnp.sum(ucol2 * k0, axis=0, keepdims=True)
        hcol = columns(hrow)
        hcol2 = jnp.concatenate([hcol, hcol], axis=1)
        kh = jnp.sum(hcol2 * k0, axis=0, keepdims=True)
        beta = cos_less * ku + sin_over * (hrow - kh)
        rot = k0 + ucol2 * beta
        own = part[y, z]
        hp = jnp.sum(hcol * own, axis=0, keepdims=True)
        cown = call[tile]
        wrow = cos_less * cown + sin_over * (jnp.sum(vs[...], axis=0) - hp)
        proj = own + ucol * wrow
        fo = 0.9 * dot(rot, mown[0]) + 0.1 * proj
        so = 0.99 * dot(rot * rot, mown[1]) + 0.01 * proj * proj
        fown[1] = so
        low[y, z] = fo / (jnp.sqrt(so) + 1e-08)

    def gather_route(name):
        kind, way, s, j = name[0], name[1], int(name[2]), int(name[3])
        main = way == "m"
        if kind in "aj":
            yy = yadd(GATHER_Y[j]) if kind == "a" else y
            zs, zr = (zadd(-s), zadd(-1 - s)) if main else (zadd(s), zadd(1 + s))
            return (yy, zs), (yy, zr), at_z(zadd(1 if main else -1))
        zz = z if kind == "h" else zadd(GATHER_Z[j])
        ys, yr = (yadd(-s), yadd(-1 - s)) if main else (y, yadd(1))
        return (ys, zz), (yr, zz), at_y(yadd(1 if main else -1))

    def gather_copy(name, to_send):
        leave, arrive, dev = gather_route(name)
        i = INDEX[name]
        rows = LO if name[0] in "ah" else HI
        yy, zz = leave if to_send else arrive

        def one():
            dst = low.at[yy, zz, rows, :]
            return copy_to(dst, dst, bulk_s.at[i], bulk_r.at[i], dev)

        return one, zz != OZ

    def gather_start(name):
        one, there = gather_copy(name, True)
        pl.when(there)(lambda: one().start())

    def gather_take(name):
        one, there = gather_copy(name, False)
        pl.when(there)(lambda: one().wait_recv())

    first_take = next(i for i, name in enumerate(GATHER_PLAN) if name[0] != ">")
    for name in GATHER_PLAN[:first_take]:
        gather_start(name[1:])

    own_rows = pl.ds(pl.multiple_of(8 * f, 8), 8)
    nb = basis[...] + (cos_less * tcol + sin_over * lifted) * unit
    new_basis[...] = nb
    left_h[...], left_l[...] = halves(nb)

    @pl.when(owner)
    def _():
        rows_out[tile] = fown[1, own_rows, :]

    columns_need = {0: {"hm00", "hn00", "hm10", "bm00", "bn00", "bm10"}}
    for s in range(4):
        columns_need[-1 - s] = {f"am{s}{j}" for j in range(4)} | {f"jm{s}0", f"bm0{s + 1}", f"bn0{s + 1}", f"bm1{s + 1}"}
    for s in range(3):
        columns_need[1 + s] = {f"an{s}{j}" for j in range(4)} | {f"jn{s}0", f"bm0{s + 5}", f"bn0{s + 5}", f"bm1{s + 5}"}
    ready, here = [], set()

    def whole_columns():
        for k in [k for k, names in columns_need.items() if here.issuperset(names)]:
            del columns_need[k]
            ready.extend(((k, 0), (k, 2)))

    def update_next():
        if not ready:
            return
        k, yy = ready.pop(0)
        zz = zadd(k)

        @pl.when(zz != OZ)
        def _():
            block = dot3((left_h[...], left_l[...]), halves(jnp.concatenate([low[yy, zz], low[yy + 1, zz]], axis=1)))
            update[yy, zz] = block[:, 0:W]
            update[yy + 1, zz] = block[:, W:]

    def o_start(i, c):
        p = (f + i) % NF
        rows = pl.ds(pl.multiple_of(8 * p, 8), 8)
        copy_to(fown.at[1, rows, :], rows_out.at[tile], o_s, o_r, {"fsdp": p}).start()
        return c

    for name in GATHER_PLAN[first_take:]:
        if name[0] == ">":
            gather_start(name[1:])
            continue
        if here:
            update_next()
            if len(here) >= 10:
                pl.when(owner)(lambda: spread(len(here) - 10, 1, o_start))
        gather_take(name)
        here.add(name)
        whole_columns()

    while ready:
        update_next()
    owners_but_me(rows_out, o_r)
    for k in range(NT):
        mixed = rows_out[k]
        second_out[:, W * k : W * k + W] = mixed
        first_out[:, W * k : W * k + W] = low[k // OZ, k % OZ, own_rows, :] * (jnp.sqrt(mixed) + 1e-08)

    p_x[2]()
    s_x[2]()
    for name in NAMES:
        one, there = gather_copy(name, True)
        pl.when(there)(lambda one=one: one().wait_send())

    @pl.when(owner)
    def _():
        wait_all(fown.at[1, pl.ds(0, R - 8), :], o_s)


def copy_out(tiles, nb, first, second, update, new_basis, first_out, second_out, sems):
    for k in range(NT):
        pltpu.make_async_copy(tiles.at[k // OZ, k % OZ], update.at[:, W * k : W * k + W], sems.at[0]).start()
    rest = [
        pltpu.make_async_copy(src, dst, sems.at[1 + i])
        for i, (src, dst) in enumerate(((nb, new_basis), (first, first_out), (second, second_out)))
    ]
    for one in rest:
        one.start()
    pltpu.make_async_copy(tiles, tiles, sems.at[0]).wait()
    for one in rest:
        one.wait()


def per_device(gradient, basis, direction, first_moment, second_moment):
    vmem = pl.BlockSpec(memory_space=pltpu.VMEM)
    anywhere = pl.BlockSpec(memory_space=pl.ANY)
    dma = pltpu.SemaphoreType.DMA
    v = lambda *shape: pltpu.VMEM(shape, F32)
    shape = lambda *s: jax.ShapeDtypeStruct(s, F32)
    rows, cols = gradient.shape
    own = first_moment.shape
    scratch = [
        v(rows, cols), v(rows, R), v(1, R), v(*own), v(*own),
        v(NY, OZ, R, W), v(NY, OZ, R, W),
        pltpu.VMEM((rows, R), BF16), pltpu.VMEM((rows, R), BF16), v(NT, 8, W),
        v(28, CUT, W), v(3, CUT, W), v(24, R - CUT, W), v(7, R - CUT, W),
        v(NT, 1, W), v(NF, 1, W), v(NT, 1, W), v(NR, 1, R), v(NF, 1, R),
        v(NT, 1, W), v(NF, 1, W), v(NR, 1, W), v(NF, 1, W),
        v(2 * NY, 8, R), v(NZ, 1, R), v(NZ, 1, R), v(NZ, 1, R), v(NY, 8, R), v(NR, 32, R),
        v(NT, 2, 8, W), v(2, R, W), v(2, R, W),
    ]
    sems = [len(NAMES), len(NAMES), 14, 14, 10]
    arrays = (gradient, basis, direction.reshape(1, R), first_moment, second_moment)
    moved = pl.pallas_call(
        kernel,
        out_shape=(shape(NY, OZ, R, W), shape(rows, R), shape(*own), shape(*own)),
        in_specs=[pl.BlockSpec(memory_space=pltpu.HBM)] * 5,
        out_specs=(vmem,) * 4,
        scratch_shapes=scratch + [dma((k,)) for k in sems],
        compiler_params=pltpu.CompilerParams(
            collective_id=0, has_side_effects=True, vmem_limit_bytes=VMEM_LIMIT
        ),
    )(*(pltpu.with_memory_space_constraint(x, pltpu.HBM) for x in arrays))
    return pl.pallas_call(
        copy_out,
        out_shape=(shape(rows, cols), shape(rows, R), shape(*own), shape(*own)),
        in_specs=[vmem] * 4,
        out_specs=(anywhere,) * 4,
        scratch_shapes=[dma((4,))],
        compiler_params=pltpu.CompilerParams(vmem_limit_bytes=12 * 1024 * 1024),
    )(*moved)


def solution(mesh):
    in_specs = (P("fsdp", "rep"), P("fsdp", None), P(), P("fsdp", "rep"), P("fsdp", "rep"))
    out_specs = (P("fsdp", "rep"), P("fsdp", None), P("fsdp", "rep"), P("fsdp", "rep"))
    return jax.shard_map(
        per_device, mesh=mesh, in_specs=in_specs, out_specs=out_specs, check_vma=False
    )
```
